256 devices in a mesh: win: 64 (over y, x, z_lo), row: 4 (over z_hi, core).
Axes of the slice: x: 4, y: 4, z: 8 (z_hi: 2, z_lo: 4; z = z_hi * 4 + z_lo), core: 2. Of those that a mesh axis runs over, the one named last changes fastest.
Arguments:
- downgoing: float32 [64, 3072, 3072], P('win', 'row'), may hold values from -64 to 64
- upgoing: float32 [64, 64, 3072], P('win'), may hold values from -6 to 6
Outputs:
- filters: float32 [256, 2, 64, 3072], P('win', None, None, 'row')
The draws below stay inside these ranges and needn't reach their ends.
All inputs are finite; a program needn't handle non-finite values.
Results may differ from the reference program's by a relative error of at most 0.00016.
Values sent between devices are 32-bit elements; how exact they have to be, the bound alone decides.
No kernel may reach another device: no remote copies, remote signals or barrier semaphores. Data moves between devices by JAX's collectives and lax.ppermute only.
A program may use at most 128 MiB of HBM per device.

```python
import math
import jax
import jax.numpy as jnp
from jax import lax

NCH = 3072
NT = 3072
NVS = 64
ITERS = 2
NWT = 64
NF = 256


def draw_downgoing(key, part):
    key_win, key_chan, key_noise = jax.random.split(key, 3)
    win_gain = jnp.exp(jax.random.uniform(key_win, (NWT, 1, 1), jnp.float32, -1.15, 1.15))
    chan_gain = jnp.exp(jax.random.uniform(key_chan, (1, NCH, 1), jnp.float32, -1.15, 1.15))
    ramp_gain = jnp.exp(0.55 * jnp.arange(NCH, dtype=jnp.float32) / NCH).reshape(1, NCH, 1)
    noise = jax.random.normal(key_noise, (NWT, NCH, NT), jnp.float32)
    return jnp.clip(noise * win_gain * chan_gain * ramp_gain, -64.0, 64.0)


def block_levels(rng, shape, shards, least, top_value):
    level, own = 1.0, jax.random.fold_in(rng, 6)
    for dim, shards_of in shards:
        draws = jnp.exp(jax.random.uniform(jax.random.fold_in(own, dim), (shards_of,), jnp.float32, least / len(shards), top_value / len(shards)))
        level = level * jnp.repeat(draws, shape[dim] // shards_of).reshape([-1 if axis == dim else 1 for axis in range(len(shape))])
    return level


def centred(stream_key, shape, scale, bound, shards=(), kind=jnp.bfloat16):
    loudness = block_levels(stream_key, shape, shards, -0.22, 0.18) if shards else 1.0
    array = jax.random.normal(stream_key, shape, jnp.float32) * scale * loudness
    return jnp.minimum(jnp.maximum(array, -bound), bound).astype(kind)


def setup_inputs(seed: int = 0) -> dict:
    arg_keys = jax.random.split(jax.random.key(seed), 3)
    return {
        "downgoing": draw_downgoing(jax.random.fold_in(arg_keys[2], 71), 0),
        "upgoing": centred(arg_keys[1], (NWT, NVS, NT), 1.0, 6.0, ((0, 64),), jnp.float32),
    }


damping = 0.5

def exact_dot(first, second):
    return jnp.dot(first, second, precision=lax.Precision.HIGHEST, preferred_element_type=jnp.float32)

def dft_table(n_samples, n_bins):
    sample_idx = jnp.arange(n_samples, dtype=jnp.int32)
    bin_idx = jnp.arange(1, n_bins + 1, dtype=jnp.int32)
    angles = (sample_idx[:, None] * bin_idx[None, :] % n_samples).astype(jnp.float32) * (2.0 * math.pi / n_samples)
    return jnp.concatenate([jnp.cos(angles), -jnp.sin(angles)], axis=1) * (1.0 / math.sqrt(n_samples))

def spectra(series, basis, n_bins):

    def one_window(window):
        return exact_dot(basis.T, window.T)
    flat = lax.map(one_window, series)
    return flat.reshape(series.shape[0], 2, n_bins, series.shape[1])

def solve_bin(down_re, down_im, up_re, up_im):
    n_chan = down_re.shape[1]
    root_chan = math.sqrt(n_chan)
    rhs_re = (exact_dot(up_re.T, down_re) + exact_dot(up_im.T, down_im)) / root_chan
    rhs_im = (exact_dot(up_im.T, down_re) - exact_dot(up_re.T, down_im)) / root_chan

    def operate(dir_re, dir_im):
        sum_re = exact_dot(dir_re, down_re.T) - exact_dot(dir_im, down_im.T)
        sum_im = exact_dot(dir_re, down_im.T) + exact_dot(dir_im, down_re.T)
        img_re = (exact_dot(sum_re, down_re) + exact_dot(sum_im, down_im)) / n_chan + damping * dir_re
        img_im = (exact_dot(sum_im, down_re) - exact_dot(sum_re, down_im)) / n_chan + damping * dir_im
        return (img_re, img_im)
    filt_re = jnp.zeros_like(rhs_re)
    filt_im = jnp.zeros_like(rhs_im)
    res_re, res_im = (rhs_re, rhs_im)
    dir_re, dir_im = (rhs_re, rhs_im)
    norm_old = lax.optimization_barrier(jnp.sum(res_re * res_re + res_im * res_im, axis=-1, keepdims=True))
    for iteration in range(ITERS):
        img_re, img_im = operate(dir_re, dir_im)
        curvature = lax.optimization_barrier(jnp.sum(dir_re * img_re + dir_im * img_im, axis=-1, keepdims=True))
        step_size = norm_old / curvature
        filt_re = filt_re + step_size * dir_re
        filt_im = filt_im + step_size * dir_im
        res_re = res_re - step_size * img_re
        res_im = res_im - step_size * img_im
        norm_new = lax.optimization_barrier(jnp.sum(res_re * res_re + res_im * res_im, axis=-1, keepdims=True))
        ratio = norm_new / norm_old
        dir_re = res_re + ratio * dir_re
        dir_im = res_im + ratio * dir_im
        norm_old = norm_new
    out_scale = math.sqrt(n_chan / down_re.shape[0])
    return jnp.stack([filt_re, filt_im]) * out_scale

def reference(downgoing, upgoing):
    basis = dft_table(NT, NF)
    spec_down = spectra(downgoing, basis, NF)
    spec_up = spectra(upgoing, basis, NF)
    by_bin = (jnp.moveaxis(spec_down, 2, 0), jnp.moveaxis(spec_up, 2, 0))

    def one_bin(pair_bin):
        return solve_bin(pair_bin[0][:, 0], pair_bin[0][:, 1], pair_bin[1][:, 0], pair_bin[1][:, 1])
    return lax.map(one_bin, by_bin)
```

```python
import math

import jax
import jax.numpy as jnp
import numpy as np
from jax import lax
from jax.experimental import pallas as pl
from jax.experimental.pallas import tpu as pltpu
from jax.sharding import PartitionSpec as P

NCH = 3072
NT = 3072
NVS = 64
NWT = 64
NF = 256
DAMPING = 0.5
QUARTER = NT // 4
LANES = 128
CH_TILE = 256
BINS = 4
ROWS_D = 2 * BINS * 6
ROWS = ROWS_D + BINS
F32 = jnp.float32
BF16 = jnp.bfloat16


def split_table(table):
    high = table.astype(BF16)
    low = (table - high.astype(np.float64)).astype(BF16)
    return np.concatenate([high, low], axis=0)


def dft_tables():
    t = np.arange(QUARTER, dtype=np.int64)
    owners = np.arange(NWT, dtype=np.int64)
    scale = 1.0 / math.sqrt(NT)

    def trig(f):
        k = 4 * owners + 1 + f
        angle = (k[:, None] * t[None, :] % NT).astype(np.float64) * (2.0 * math.pi / NT)
        return np.cos(angle) * scale, np.sin(angle) * scale

    odd = []
    for f, sign in ((0, 1.0), (2, -1.0)):
        cos, sin = trig(f)
        odd.append(np.concatenate([cos, -sign * sin], axis=1))
        odd.append(np.concatenate([-sin, -sign * cos], axis=1))
    even = []
    for f in (1, 3):
        cos, sin = trig(f)
        even.append(split_table(np.concatenate([cos, -sin], axis=0)))
    return split_table(np.concatenate(odd, axis=0)), even[0], even[1]


def split(x):
    high = x.astype(BF16)
    return high, (x - high.astype(F32)).astype(BF16)


def dot_nt(a, b):
    return lax.dot_general(a, b, (((1,), (1,)), ((), ())), preferred_element_type=F32)


def dot_nn(a, b):
    return lax.dot_general(a, b, (((1,), (0,)), ((), ())), preferred_element_type=F32)


def table_dot(table_ref, y):
    half = table_ref.shape[0] // 2
    high, low = split(y)
    both = dot_nt(table_ref[...], high)
    return both[:half] + both[half:] + dot_nt(table_ref[pl.ds(0, half), :], low)


def dft_kernel(x_ref, up_ref, todd_ref, t1_ref, t3_ref, o_ref):
    step = pl.program_id(0)

    def spectra(read):
        x0, x1, x2, x3 = (read(q) for q in range(4))
        sum0, sum1, dif0, dif1 = x0 + x2, x1 + x3, x0 - x2, x1 - x3
        odd = table_dot(todd_ref, jnp.concatenate([dif0, dif1], axis=1))
        even1 = table_dot(t1_ref, sum0 - sum1)
        even3 = table_dot(t3_ref, sum0 + sum1)
        return (
            (odd[0:64], odd[64:128]),
            (even1[0:64], even1[64:128]),
            (odd[128:192], odd[192:256]),
            (even3[0:64], even3[64:128]),
        )

    spec = spectra(lambda q: x_ref[:, pl.ds(q * QUARTER, QUARTER)])
    for f in range(BINS):
        for ri in range(2):
            for j in range(CH_TILE // LANES):
                row = (f * 2 + ri) * 6 + step * (CH_TILE // LANES) + j
                o_ref[pl.ds(row, NWT, stride=ROWS), :] = spec[f][ri][:, j * LANES : (j + 1) * LANES]

    @pl.when(step == pl.num_programs(0) - 1)
    def _():
        def read(q):
            part = up_ref[:, pl.ds(q * QUARTER, QUARTER)]
            return jnp.concatenate([part, part], axis=0)

        spec_up = spectra(read)
        left = lax.broadcasted_iota(jnp.int32, (NWT, LANES), 1) < 64
        for f in range(BINS):
            o_ref[pl.ds(ROWS_D + f, NWT, stride=ROWS), :] = jnp.where(left, spec_up[f][0], spec_up[f][1])


def dft(x, up):
    todd, t1, t3 = dft_tables()
    steps = x.shape[0] // CH_TILE

    def whole(a):
        return pl.BlockSpec(a.shape, lambda i: (0, 0), pipeline_mode=pl.Buffered(1))

    return pl.pallas_call(
        dft_kernel,
        out_shape=jax.ShapeDtypeStruct((NWT * ROWS, LANES), F32),
        grid=(steps,),
        in_specs=[
            pl.BlockSpec((CH_TILE, NT), lambda i: (i, 0)),
            whole(up),
            whole(todd),
            whole(t1),
            whole(t3),
        ],
        out_specs=pl.BlockSpec((NWT * ROWS, LANES), lambda i: (0, 0)),
        compiler_params=pltpu.CompilerParams(vmem_limit_bytes=50 << 20),
        cost_estimate=pl.CostEstimate(flops=3 * 10**9, bytes_accessed=15 * 10**6, transcendentals=0),
        name="dft",
    )(x, up, jnp.asarray(todd), jnp.asarray(t1), jnp.asarray(t3))


def bin_rows(r_ref, f, ri):
    return jnp.concatenate(
        [r_ref[pl.ds((f * 2 + ri) * 6 + ct, NWT, stride=ROWS), :] for ct in range(6)], axis=1
    )


def gram_kernel(r_ref, g_ref):
    lane = lax.broadcasted_iota(jnp.int32, (NWT, LANES), 1)
    row = lax.broadcasted_iota(jnp.int32, (NWT, LANES), 0)
    upper = row <= lane % 64
    left = lane < 64
    packed = []
    for f in range(BINS):
        re_h, re_l = split(bin_rows(r_ref, f, 0))
        im_h, im_l = split(bin_rows(r_ref, f, 1))
        lhs_h = jnp.concatenate([re_h, im_h], axis=1)
        lhs_l = jnp.concatenate([re_l, im_l], axis=1)
        rhs_h = jnp.concatenate([lhs_h, jnp.concatenate([im_h, -re_h], axis=1)], axis=0)
        rhs_l = jnp.concatenate([lhs_l, jnp.concatenate([im_l, -re_l], axis=1)], axis=0)
        both = dot_nt(lhs_h, rhs_h) + dot_nt(lhs_h, rhs_l) + dot_nt(lhs_l, rhs_h)
        swapped = pltpu.roll(both, 64, 1)
        packed.append(jnp.where(upper == left, both, swapped))
    for pair in range(BINS // 2):
        g_ref[pair] = jnp.where(left, packed[2 * pair], packed[2 * pair + 1])


def gram(recv):
    return pl.pallas_call(
        gram_kernel,
        out_shape=jax.ShapeDtypeStruct((BINS // 2, NWT, LANES), F32),
        compiler_params=pltpu.CompilerParams(vmem_limit_bytes=40 << 20),
        cost_estimate=pl.CostEstimate(flops=3 * 10**8, bytes_accessed=2 * 10**6, transcendentals=0),
        name="gram",
    )(recv)


def dot3(a, b_h, b_l):
    a_h, a_l = split(a)
    return dot_nn(a_h, b_h) + dot_nn(a_l, b_h) + dot_nn(a_h, b_l)


def row_dot(a, b):
    return jnp.sum(a * b, axis=1, keepdims=True)


def solve_kernel(r_ref, ga_ref, gb_ref, o_ref):
    lane = lax.broadcasted_iota(jnp.int32, (NWT, LANES), 1)
    row = lax.broadcasted_iota(jnp.int32, (NWT, LANES), 0)
    col = lane % 64
    left = lane < 64
    grams = []
    for pair in range(BINS // 2):
        packed = ga_ref[pair] + gb_ref[pair]
        turned = jnp.concatenate([packed, packed], axis=0).T
        other = pltpu.roll(packed, 64, 1)
        for half in range(2):
            here = jnp.where(left == (half == 0), packed, other)
            there = turned[half * 64 : half * 64 + 64]
            real = jnp.where(row <= col, here, there)
            imag = jnp.where(row > col, here, jnp.where(row == col, 0.0, -there))
            top = jnp.where(left, real, imag)
            bottom = jnp.where(left, -imag, real)
            grams.append(split(jnp.concatenate([top, bottom], axis=0)))
    starts = []
    for f in range(BINS):
        up = r_ref[pl.ds(ROWS_D + f, NWT, stride=ROWS), :]
        turned = jnp.concatenate([up, up], axis=0).T
        starts.append(jnp.where(left, turned[:64], turned[64:]) * (1.0 / math.sqrt(NCH)))

    def times_gram(ys):
        return [dot3(y, *g) for y, g in zip(ys, grams)]

    res = starts
    res_g = times_gram(res)
    res_gg = times_gram(res_g)
    for f in range(BINS):
        dir0, dir0_g, dir0_gg = res[f], res_g[f], res_gg[f]
        norm0 = row_dot(dir0, dir0_g)
        img = dir0_g * (1.0 / NCH) + DAMPING * dir0
        img_g = dir0_gg * (1.0 / NCH) + DAMPING * dir0_g
        step0 = norm0 / row_dot(dir0_g, img)
        res1 = dir0 - step0 * img
        res1_g = dir0_g - step0 * img_g
        norm1 = row_dot(res1, res1_g)
        ratio = norm1 / norm0
        dir1 = res1 + ratio * dir0
        dir1_g = res1_g + ratio * dir0_g
        img1 = dir1_g * (1.0 / NCH) + DAMPING * dir1
        step1 = norm1 / row_dot(dir1_g, img1)
        filt = (step0 * dir0 + step1 * dir1) * math.sqrt(NCH / NWT)
        turned = pltpu.roll(filt, 64, 1)
        lhs_h, lhs_l = split(jnp.concatenate([filt, jnp.where(left, turned, -turned)], axis=0))
        rhs_h, rhs_l = split(jnp.concatenate([bin_rows(r_ref, f, 0), bin_rows(r_ref, f, 1)], axis=0))
        out = dot_nn(lhs_h, rhs_h) + dot_nn(lhs_l, rhs_h) + dot_nn(lhs_h, rhs_l)
        o_ref[f, 0] = out[:64]
        o_ref[f, 1] = out[64:]


def solve(recv, gram_a, gram_b, channels):
    return pl.pallas_call(
        solve_kernel,
        out_shape=jax.ShapeDtypeStruct((BINS, 2, NVS, channels), F32),
        compiler_params=pltpu.CompilerParams(vmem_limit_bytes=40 << 20),
        cost_estimate=pl.CostEstimate(flops=3 * 10**8, bytes_accessed=4 * 10**6, transcendentals=0),
        name="solve",
    )(recv, gram_a, gram_b)


CORE_PAIRS = [(0, 1), (1, 0), (2, 3), (3, 2)]
FAR_PAIRS = [(0, 2), (2, 0), (1, 3), (3, 1)]


def body(downgoing, upgoing):
    channels = downgoing.shape[1]
    sent = dft(downgoing[0], upgoing[0])
    sent = sent.reshape(NWT, ROWS // 4, 4, LANES)
    recv = lax.all_to_all(sent, "win", split_axis=0, concat_axis=0, tiled=True)
    recv = recv.reshape(NWT * ROWS, LANES)
    part = gram(recv)
    chip = part + lax.ppermute(part, "row", CORE_PAIRS)
    far = lax.ppermute(chip, "row", FAR_PAIRS)
    return solve(recv, chip, far, channels)


def solution(mesh):
    in_specs = (P("win", "row", None), P("win", None, None))
    out_specs = P("win", None, None, "row")
    return jax.shard_map(body, mesh=mesh, in_specs=in_specs, out_specs=out_specs, check_vma=False)
```

```python
import math

import jax
import jax.numpy as jnp
import numpy as np
from jax import lax
from jax.experimental import pallas as pl
from jax.experimental.pallas import tpu as pltpu
from jax.sharding import PartitionSpec as P

NCH = 3072
NT = 3072
NVS = 64
NWT = 64
NF = 256
DAMPING = 0.5
QUARTER = NT // 4
LANES = 128
CH_TILE = 256
FOLD_ROWS = 16
VMEM_LIMIT = 60 << 20
BINS = 4
ROWS_D = 2 * BINS * 6
ROWS = ROWS_D + BINS
F32 = jnp.float32
BF16 = jnp.bfloat16


def split_table(table):
    high = table.astype(BF16)
    low = (table - high.astype(np.float64)).astype(BF16)
    return np.concatenate([high, low], axis=0)


def dft_tables():
    t = np.arange(QUARTER, dtype=np.int64)
    owners = np.arange(NWT, dtype=np.int64)
    scale = 1.0 / math.sqrt(NT)

    def trig(f):
        k = 4 * owners + 1 + f
        angle = (k[:, None] * t[None, :] % NT).astype(np.float64) * (2.0 * math.pi / NT)
        return np.cos(angle) * scale, np.sin(angle) * scale

    odd = []
    for f, sign in ((0, 1.0), (2, -1.0)):
        cos, sin = trig(f)
        odd.append(np.concatenate([cos, -sign * sin], axis=1))
        odd.append(np.concatenate([-sin, -sign * cos], axis=1))
    even = []
    for f in (1, 3):
        cos, sin = trig(f)
        even.append(split_table(np.concatenate([cos, -sin], axis=0)))
    return np.concatenate([split_table(np.concatenate(odd, axis=0)), np.concatenate(even, axis=0)], axis=1)


def split(x):
    high = x.astype(BF16)
    return high, (x - high.astype(F32)).astype(BF16)


def dot_nt(a, b):
    return lax.dot_general(a, b, (((1,), (1,)), ((), ())), preferred_element_type=F32)


def dot_nn(a, b):
    return lax.dot_general(a, b, (((1,), (0,)), ((), ())), preferred_element_type=F32)


def table_dot(table, high, low):
    half = table.shape[0] // 2
    both = dot_nt(table, high)
    return both[:half] + both[half:] + dot_nt(table[:half], low)


def dft_kernel(x_hbm, up_hbm, table_hbm, o_ref, x_ref, table_ref, high_ref, low_ref, x_sem, up_sem, table_sem):
    channels = x_hbm.shape[0]
    tiles = channels // CH_TILE

    def x_copy(i):
        rows = pl.ds(pl.multiple_of(i * CH_TILE, CH_TILE), CH_TILE)
        return pltpu.make_async_copy(x_hbm.at[rows], x_ref.at[rows], x_sem.at[i])

    up_copy = pltpu.make_async_copy(up_hbm, x_ref.at[pl.ds(channels, NVS)], up_sem)
    table_copy = pltpu.make_async_copy(table_hbm, table_ref, table_sem)
    x_copy(0).start()
    table_copy.start()
    x_copy(1).start()

    def fold(first, count):
        for r in range(0, count, FOLD_ROWS):
            x0, x1, x2, x3 = (
                x_ref[pl.ds(first + r, FOLD_ROWS), pl.ds(q * QUARTER, QUARTER)] for q in range(4)
            )
            sum0, sum1 = x0 + x2, x1 + x3
            for k, y in enumerate((x0 - x2, x1 - x3, sum0 - sum1, sum0 + sum1)):
                high, low = split(y)
                high_ref[pl.ds(r, FOLD_ROWS), pl.ds(k * QUARTER, QUARTER)] = high
                low_ref[pl.ds(r, FOLD_ROWS), pl.ds(k * QUARTER, QUARTER)] = low

    def spectra(count):
        def part(rows, table_col, col, size):
            table = table_ref[pl.ds(*rows), pl.ds(table_col, size)]
            cut = (pl.ds(0, count), pl.ds(col, size))
            return table_dot(table, high_ref[cut], low_ref[cut])

        odd = part((0, 512), 0, 0, 2 * QUARTER)
        even1 = part((0, 256), 2 * QUARTER, 2 * QUARTER, QUARTER)
        even3 = part((256, 256), 2 * QUARTER, 3 * QUARTER, QUARTER)
        return (
            (odd[0:64], odd[64:128]),
            (even1[0:64], even1[64:128]),
            (odd[128:192], odd[192:256]),
            (even3[0:64], even3[64:128]),
        )

    @pl.loop(0, tiles)
    def _(i):
        x_copy(i).wait()

        @pl.when(i + 2 < tiles)
        def _():
            x_copy(i + 2).start()

        @pl.when(i + 2 == tiles)
        def _():
            up_copy.start()

        fold(pl.multiple_of(i * CH_TILE, CH_TILE), CH_TILE)

        @pl.when(i == 0)
        def _():
            table_copy.wait()

        spec = spectra(CH_TILE)
        for f in range(BINS):
            for ri in range(2):
                for j in range(CH_TILE // LANES):
                    row = (f * 2 + ri) * 6 + i * (CH_TILE // LANES) + j
                    o_ref[pl.ds(row, NWT, stride=ROWS), :] = spec[f][ri][:, j * LANES : (j + 1) * LANES]

    up_copy.wait()
    fold(channels, NVS)
    for ref in (high_ref, low_ref):
        ref[pl.ds(NVS, NVS)] = ref[pl.ds(0, NVS)]
    spec_up = spectra(2 * NVS)
    left = lax.broadcasted_iota(jnp.int32, (NWT, LANES), 1) < 64
    for f in range(BINS):
        o_ref[pl.ds(ROWS_D + f, NWT, stride=ROWS), :] = jnp.where(left, spec_up[f][0], spec_up[f][1])


def dft(x, up):
    table = dft_tables()
    channels = x.shape[0]
    in_hbm = pl.BlockSpec(memory_space=pltpu.HBM)
    return pl.pallas_call(
        dft_kernel,
        out_shape=pltpu.VMEM((NWT * ROWS, LANES), F32),
        in_specs=[in_hbm, in_hbm, in_hbm],
        scratch_shapes=[
            pltpu.VMEM((channels + NVS, NT), F32),
            pltpu.VMEM(table.shape, BF16),
            pltpu.VMEM((CH_TILE, NT), BF16),
            pltpu.VMEM((CH_TILE, NT), BF16),
            pltpu.SemaphoreType.DMA((channels // CH_TILE,)),
            pltpu.SemaphoreType.DMA,
            pltpu.SemaphoreType.DMA,
        ],
        compiler_params=pltpu.CompilerParams(vmem_limit_bytes=VMEM_LIMIT),
        cost_estimate=pl.CostEstimate(flops=3 * 10**9, bytes_accessed=15 * 10**6, transcendentals=0),
        name="dft",
    )(x, up, jnp.asarray(table))


def bin_rows(r_ref, f, ri):
    return jnp.concatenate(
        [r_ref[pl.ds((f * 2 + ri) * 6 + ct, NWT, stride=ROWS), :] for ct in range(6)], axis=1
    )


def bin_matrix(r_ref, f):
    return split(jnp.concatenate([bin_rows(r_ref, f, 0), bin_rows(r_ref, f, 1)], axis=0))


def gram_kernel(r_ref, g_ref):
    lane = lax.broadcasted_iota(jnp.int32, (NWT, LANES), 1)
    row = lax.broadcasted_iota(jnp.int32, (NWT, LANES), 0)
    upper = row <= lane % 64
    left = lane < 64
    packed = []
    for f in range(BINS):
        high, low = bin_matrix(r_ref, f)
        both = dot_nt(jnp.concatenate([high, low], axis=0), high)
        cross = both[LANES:]
        total = both[:LANES] + cross + cross.T
        below = pltpu.roll(total[64:], 64, 1)
        both = total[:64] + jnp.where(left, below, -below)
        swapped = pltpu.roll(both, 64, 1)
        packed.append(jnp.where(upper == left, both, swapped))
    for pair in range(BINS // 2):
        g_ref[pair] = jnp.where(left, packed[2 * pair], packed[2 * pair + 1])


def gram(recv):
    return pl.pallas_call(
        gram_kernel,
        out_shape=jax.ShapeDtypeStruct((BINS // 2, NWT, LANES), F32),
        compiler_params=pltpu.CompilerParams(vmem_limit_bytes=40 << 20),
        cost_estimate=pl.CostEstimate(flops=3 * 10**8, bytes_accessed=2 * 10**6, transcendentals=0),
        name="gram",
    )(recv)


def prep_kernel(r_ref, high_ref, low_ref, start_ref):
    left = lax.broadcasted_iota(jnp.int32, (NWT, LANES), 1) < 64
    for f in range(BINS):
        high_ref[f], low_ref[f] = bin_matrix(r_ref, f)
        up = r_ref[pl.ds(ROWS_D + f, NWT, stride=ROWS), :]
        turned = jnp.concatenate([up, up], axis=0).T
        start_ref[f] = jnp.where(left, turned[:64], turned[64:]) * (1.0 / math.sqrt(NCH))


def prep(recv, channels):
    matrices = pltpu.VMEM((BINS, 2 * NWT, channels), BF16)
    return pl.pallas_call(
        prep_kernel,
        out_shape=(matrices, matrices, pltpu.VMEM((BINS, NVS, LANES), F32)),
        compiler_params=pltpu.CompilerParams(vmem_limit_bytes=40 << 20),
        cost_estimate=pl.CostEstimate(flops=10**7, bytes_accessed=4 * 10**6, transcendentals=0),
        name="prep",
    )(recv)


def dot3(a, b_h, b_l):
    a_h, a_l = split(a)
    return dot_nn(a_h, b_h) + dot_nn(a_l, b_h) + dot_nn(a_h, b_l)


def row_dot(a, b):
    return jnp.sum(a * b, axis=1, keepdims=True)


def solve_kernel(high_ref, low_ref, start_ref, ga_ref, gb_ref, o_ref):
    lane = lax.broadcasted_iota(jnp.int32, (NWT, LANES), 1)
    row = lax.broadcasted_iota(jnp.int32, (NWT, LANES), 0)
    col = lane % 64
    left = lane < 64
    grams = []
    for pair in range(BINS // 2):
        packed = ga_ref[pair] + gb_ref[pair]
        turned = jnp.concatenate([packed, packed], axis=0).T
        other = pltpu.roll(packed, 64, 1)
        for half in range(2):
            here = jnp.where(left == (half == 0), packed, other)
            there = turned[half * 64 : half * 64 + 64]
            real = jnp.where(row <= col, here, there)
            imag = jnp.where(row > col, here, jnp.where(row == col, 0.0, -there))
            top = jnp.where(left, real, imag)
            bottom = jnp.where(left, -imag, real)
            grams.append(split(jnp.concatenate([top, bottom], axis=0)))
    starts = [start_ref[f] for f in range(BINS)]

    def times_gram(ys):
        return [dot3(y, *g) for y, g in zip(ys, grams)]

    res = starts
    res_g = times_gram(res)
    res_gg = times_gram(res_g)
    for f in range(BINS):
        dir0, dir0_g, dir0_gg = res[f], res_g[f], res_gg[f]
        norm0 = row_dot(dir0, dir0_g)
        img = dir0_g * (1.0 / NCH) + DAMPING * dir0
        img_g = dir0_gg * (1.0 / NCH) + DAMPING * dir0_g
        step0 = norm0 / row_dot(dir0_g, img)
        res1 = dir0 - step0 * img
        res1_g = dir0_g - step0 * img_g
        norm1 = row_dot(res1, res1_g)
        ratio = norm1 / norm0
        dir1 = res1 + ratio * dir0
        dir1_g = res1_g + ratio * dir0_g
        img1 = dir1_g * (1.0 / NCH) + DAMPING * dir1
        step1 = norm1 / row_dot(dir1_g, img1)
        filt = (step0 * dir0 + step1 * dir1) * math.sqrt(NCH / NWT)
        turned = pltpu.roll(filt, 64, 1)
        lhs_h, lhs_l = split(jnp.concatenate([filt, jnp.where(left, turned, -turned)], axis=0))
        both = dot_nn(jnp.concatenate([lhs_h, lhs_l], axis=0), high_ref[f])
        out = both[:LANES] + both[LANES:] + dot_nn(lhs_h, low_ref[f])
        o_ref[f, 0] = out[:64]
        o_ref[f, 1] = out[64:]


def solve(prepared, gram_a, gram_b, channels):
    return pl.pallas_call(
        solve_kernel,
        out_shape=jax.ShapeDtypeStruct((BINS, 2, NVS, channels), F32),
        compiler_params=pltpu.CompilerParams(vmem_limit_bytes=40 << 20),
        cost_estimate=pl.CostEstimate(flops=3 * 10**8, bytes_accessed=4 * 10**6, transcendentals=0),
        name="solve",
    )(*prepared, gram_a, gram_b)


CORE_PAIRS = [(0, 1), (1, 0), (2, 3), (3, 2)]
FAR_PAIRS = [(0, 2), (2, 0), (1, 3), (3, 1)]


def body(downgoing, upgoing):
    channels = downgoing.shape[1]
    sent = dft(downgoing[0], upgoing[0])
    sent = sent.reshape(NWT, ROWS // 4, 4, LANES)
    recv = lax.all_to_all(sent, "win", split_axis=0, concat_axis=0, tiled=True)
    recv = recv.reshape(NWT * ROWS, LANES)
    part = gram(recv)
    chip = part + lax.ppermute(part, "row", CORE_PAIRS)
    far = lax.ppermute(chip, "row", FAR_PAIRS)
    return solve(prep(recv, channels), chip, far, channels)


def solution(mesh):
    in_specs = (P("win", "row", None), P("win", None, None))
    out_specs = P("win", None, None, "row")
    return jax.shard_map(body, mesh=mesh, in_specs=in_specs, out_specs=out_specs, check_vma=False)
```

```python
import math

import jax
import jax.numpy as jnp
import numpy as np
from jax import lax
from jax.experimental import pallas as pl
from jax.experimental.pallas import tpu as pltpu
from jax.sharding import PartitionSpec as P

NCH = 3072
NT = 3072
NVS = 64
NWT = 64
NF = 256
DAMPING = 0.5
QUARTER = NT // 4
EIGHTH = NT // 8
LANES = 128
CH_TILE = 256
FOLD_ROWS = 16
VMEM_LIMIT = 60 << 20
BINS = 4
ROWS_D = 2 * BINS * 6
ROWS = ROWS_D + BINS
F32 = jnp.float32
BF16 = jnp.bfloat16


def split_table(table):
    high = table.astype(BF16)
    low = (table - high.astype(np.float64)).astype(BF16)
    return np.concatenate([high, low], axis=0)


def dft_tables():
    scale = 1.0 / math.sqrt(NT)

    def trig(f, owners, samples):
        k = 4 * np.arange(NWT, dtype=np.int64)[owners] + 1 + f
        t = np.arange(samples, dtype=np.int64)
        angle = (k[:, None] * t[None, :] % NT).astype(np.float64) * (2.0 * math.pi / NT)
        return np.cos(angle) * scale, np.sin(angle) * scale

    tables = []
    for first in (0, 1):
        rows = []
        for f, sign, parity in ((0, 1.0, first), (2, -1.0, 1 - first)):
            cos, sin = trig(f, slice(parity, None, 2), EIGHTH)
            rows.append(np.concatenate([cos, -sign * sin], axis=1))
            rows.append(np.concatenate([-sin, -sign * cos], axis=1))
        tables.append(split_table(np.concatenate(rows, axis=0)))
    for f in (1, 3):
        cos, sin = trig(f, slice(None), QUARTER)
        tables.append(split_table(np.concatenate([cos, -sin], axis=0)))
    return np.concatenate(tables, axis=0)


CLASS_ROWS = [
    [(f, ri, first if f == 0 else 1 - first, 2) for f in (0, 2) for ri in range(2)] for first in (0, 1)
] + [[(f, ri, 0, 1) for ri in range(2)] for f in (1, 3)]


def split(x):
    high = x.astype(BF16)
    return high, (x - high.astype(F32)).astype(BF16)


def dot_nt(a, b):
    return lax.dot_general(a, b, (((1,), (1,)), ((), ())), preferred_element_type=F32)


def dot_nn(a, b):
    return lax.dot_general(a, b, (((1,), (0,)), ((), ())), preferred_element_type=F32)


def table_dot(table, high, low):
    half = table.shape[0] // 2
    both = dot_nt(table, high)
    return both[:half] + both[half:] + dot_nt(table[:half], low)


def dft_kernel(x_hbm, up_hbm, table_hbm, o_ref, x_ref, table_ref, high_ref, low_ref, x_sem, up_sem, table_sem):
    channels = x_hbm.shape[0]
    tiles = channels // CH_TILE

    def x_copy(i):
        rows = pl.ds(pl.multiple_of(i * CH_TILE, CH_TILE), CH_TILE)
        return pltpu.make_async_copy(x_hbm.at[rows], x_ref.at[rows], x_sem.at[i])

    up_copy = pltpu.make_async_copy(up_hbm, x_ref.at[pl.ds(channels, NVS)], up_sem)
    table_copy = pltpu.make_async_copy(table_hbm, table_ref, table_sem)
    x_copy(0).start()
    table_copy.start()
    x_copy(1).start()

    def fold(first, count):
        for r in range(0, count, FOLD_ROWS):
            x0, x1, x2, x3 = (
                x_ref[pl.ds(first + r, FOLD_ROWS), pl.ds(q * QUARTER, QUARTER)] for q in range(4)
            )
            sum0, sum1, dif0, dif1 = x0 + x2, x1 + x3, x0 - x2, x1 - x3
            near0, far0, near1, far1 = dif0[:, :EIGHTH], dif0[:, EIGHTH:], dif1[:, :EIGHTH], dif1[:, EIGHTH:]
            turn0, turn1 = (far0 - far1) * math.sqrt(0.5), (far0 + far1) * math.sqrt(0.5)
            folded = (near0 + turn0, near1 + turn1, near0 - turn0, near1 - turn1, sum0 - sum1, sum0 + sum1)
            col = 0
            for y in folded:
                cut = (pl.ds(r, FOLD_ROWS), pl.ds(col, y.shape[1]))
                high_ref[cut], low_ref[cut] = split(y)
                col += y.shape[1]

    def table(c):
        return table_ref[pl.ds(c * 2 * LANES, 2 * LANES), :]

    def owner_rows(row, owner, step):
        return pl.ds(row + owner * ROWS, NWT // step, stride=step * ROWS)

    @pl.loop(0, tiles)
    def _(i):
        x_copy(i).wait()

        @pl.when(i + 2 < tiles)
        def _():
            x_copy(i + 2).start()

        @pl.when(i + 2 == tiles)
        def _():
            up_copy.start()

        fold(pl.multiple_of(i * CH_TILE, CH_TILE), CH_TILE)

        @pl.when(i == 0)
        def _():
            table_copy.wait()

        for c, runs in enumerate(CLASS_ROWS):
            cut = (slice(None), pl.ds(c * QUARTER, QUARTER))
            spec = table_dot(table(c), high_ref[cut], low_ref[cut])
            start = 0
            for f, ri, owner, step in runs:
                for j in range(CH_TILE // LANES):
                    row = (f * 2 + ri) * 6 + i * (CH_TILE // LANES) + j
                    o_ref[owner_rows(row, owner, step), :] = spec[
                        start : start + NWT // step, j * LANES : (j + 1) * LANES
                    ]
                start += NWT // step

    up_copy.wait()
    fold(channels, NVS)
    for c, runs in enumerate(CLASS_ROWS):
        cut = (pl.ds(0, NVS), pl.ds(c * QUARTER, QUARTER))
        both = dot_nt(jnp.concatenate([high_ref[cut], low_ref[cut]], axis=0), table(c))
        spec = both[:NVS, :LANES] + both[:NVS, LANES:] + both[NVS:, :LANES]
        turned = jnp.concatenate([spec, spec], axis=0).T
        start = 0
        for (f, _, owner, step), _ in zip(runs[::2], runs[1::2]):
            count = NWT // step
            left = lax.broadcasted_iota(jnp.int32, (count, LANES), 1) < 64
            o_ref[owner_rows(ROWS_D + f, owner, step), :] = jnp.where(
                left, turned[start : start + count], turned[start + count : start + 2 * count]
            )
            start += 2 * count


def dft(x, up):
    table = dft_tables()
    channels = x.shape[0]
    in_hbm = pl.BlockSpec(memory_space=pltpu.HBM)
    return pl.pallas_call(
        dft_kernel,
        out_shape=pltpu.VMEM((NWT * ROWS, LANES), F32),
        in_specs=[in_hbm, in_hbm, in_hbm],
        scratch_shapes=[
            pltpu.VMEM((channels + NVS, NT), F32),
            pltpu.VMEM(table.shape, BF16),
            pltpu.VMEM((CH_TILE, NT), BF16),
            pltpu.VMEM((CH_TILE, NT), BF16),
            pltpu.SemaphoreType.DMA((channels // CH_TILE,)),
            pltpu.SemaphoreType.DMA,
            pltpu.SemaphoreType.DMA,
        ],
        compiler_params=pltpu.CompilerParams(vmem_limit_bytes=VMEM_LIMIT),
        cost_estimate=pl.CostEstimate(flops=3 * 10**9, bytes_accessed=15 * 10**6, transcendentals=0),
        name="dft",
    )(x, up, jnp.asarray(table))


def bin_rows(r_ref, f, ri):
    return jnp.concatenate(
        [r_ref[pl.ds((f * 2 + ri) * 6 + ct, NWT, stride=ROWS), :] for ct in range(6)], axis=1
    )


def bin_matrix(r_ref, f):
    return split(jnp.concatenate([bin_rows(r_ref, f, 0), bin_rows(r_ref, f, 1)], axis=0))


def gram_kernel(r_ref, g_ref):
    lane = lax.broadcasted_iota(jnp.int32, (NWT, LANES), 1)
    row = lax.broadcasted_iota(jnp.int32, (NWT, LANES), 0)
    upper = row <= lane % 64
    left = lane < 64
    packed = []
    for f in range(BINS):
        high, low = bin_matrix(r_ref, f)
        both = dot_nt(jnp.concatenate([high, low], axis=0), high)
        cross = both[LANES:]
        total = both[:LANES] + cross + cross.T
        below = pltpu.roll(total[64:], 64, 1)
        both = total[:64] + jnp.where(left, below, -below)
        swapped = pltpu.roll(both, 64, 1)
        packed.append(jnp.where(upper == left, both, swapped))
    for pair in range(BINS // 2):
        g_ref[pair] = jnp.where(left, packed[2 * pair], packed[2 * pair + 1])


def gram(recv):
    return pl.pallas_call(
        gram_kernel,
        out_shape=jax.ShapeDtypeStruct((BINS // 2, NWT, LANES), F32),
        compiler_params=pltpu.CompilerParams(vmem_limit_bytes=40 << 20),
        cost_estimate=pl.CostEstimate(flops=3 * 10**8, bytes_accessed=2 * 10**6, transcendentals=0),
        name="gram",
    )(recv)


def prep_kernel(r_ref, high_ref, low_ref, start_ref):
    left = lax.broadcasted_iota(jnp.int32, (NWT, LANES), 1) < 64
    for f in range(BINS):
        high_ref[f], low_ref[f] = bin_matrix(r_ref, f)
        up = r_ref[pl.ds(ROWS_D + f, NWT, stride=ROWS), :]
        turned = jnp.concatenate([up, up], axis=0).T
        start_ref[f] = jnp.where(left, turned[:64], turned[64:]) * (1.0 / math.sqrt(NCH))


def prep(recv, channels):
    matrices = pltpu.VMEM((BINS, 2 * NWT, channels), BF16)
    return pl.pallas_call(
        prep_kernel,
        out_shape=(matrices, matrices, pltpu.VMEM((BINS, NVS, LANES), F32)),
        compiler_params=pltpu.CompilerParams(vmem_limit_bytes=40 << 20),
        cost_estimate=pl.CostEstimate(flops=10**7, bytes_accessed=4 * 10**6, transcendentals=0),
        name="prep",
    )(recv)


def dot3(a, b_h, b_l):
    a_h, a_l = split(a)
    return dot_nn(a_h, b_h) + dot_nn(a_l, b_h) + dot_nn(a_h, b_l)


def row_dot(a, b):
    return jnp.sum(a * b, axis=1, keepdims=True)


def solve_kernel(high_ref, low_ref, start_ref, ga_ref, gb_ref, o_hbm, o_ref, o_sem):
    lane = lax.broadcasted_iota(jnp.int32, (NWT, LANES), 1)
    row = lax.broadcasted_iota(jnp.int32, (NWT, LANES), 0)
    col = lane % 64
    left = lane < 64
    grams = []
    for pair in range(BINS // 2):
        packed = ga_ref[pair] + gb_ref[pair]
        turned = jnp.concatenate([packed, packed], axis=0).T
        other = pltpu.roll(packed, 64, 1)
        for half in range(2):
            here = jnp.where(left == (half == 0), packed, other)
            there = turned[half * 64 : half * 64 + 64]
            real = jnp.where(row <= col, here, there)
            imag = jnp.where(row > col, here, jnp.where(row == col, 0.0, -there))
            top = jnp.where(left, real, imag)
            bottom = jnp.where(left, -imag, real)
            grams.append(split(jnp.concatenate([top, bottom], axis=0)))
    starts = [start_ref[f] for f in range(BINS)]

    def times_gram(ys):
        return [dot3(y, *g) for y, g in zip(ys, grams)]

    res = starts
    res_g = times_gram(res)
    res_gg = times_gram(res_g)
    copies = []
    for f in range(BINS):
        dir0, dir0_g, dir0_gg = res[f], res_g[f], res_gg[f]
        norm0 = row_dot(dir0, dir0_g)
        img = dir0_g * (1.0 / NCH) + DAMPING * dir0
        img_g = dir0_gg * (1.0 / NCH) + DAMPING * dir0_g
        step0 = norm0 / row_dot(dir0_g, img)
        res1 = dir0 - step0 * img
        res1_g = dir0_g - step0 * img_g
        norm1 = row_dot(res1, res1_g)
        ratio = norm1 / norm0
        dir1 = res1 + ratio * dir0
        dir1_g = res1_g + ratio * dir0_g
        img1 = dir1_g * (1.0 / NCH) + DAMPING * dir1
        step1 = norm1 / row_dot(dir1_g, img1)
        filt = (step0 * dir0 + step1 * dir1) * math.sqrt(NCH / NWT)
        turned = pltpu.roll(filt, 64, 1)
        lhs_h, lhs_l = split(jnp.concatenate([filt, jnp.where(left, turned, -turned)], axis=0))
        both = dot_nn(jnp.concatenate([lhs_h, lhs_l], axis=0), high_ref[f])
        out = both[:LANES] + both[LANES:] + dot_nn(lhs_h, low_ref[f])
        o_ref[f, 0] = out[:64]
        o_ref[f, 1] = out[64:]
        copies.append(pltpu.make_async_copy(o_ref.at[f], o_hbm.at[f], o_sem.at[f]))
        copies[f].start()
    for copy in copies:
        copy.wait()


def solve(prepared, gram_a, gram_b, channels):
    return pl.pallas_call(
        solve_kernel,
        out_shape=jax.ShapeDtypeStruct((BINS, 2, NVS, channels), F32),
        out_specs=pl.BlockSpec(memory_space=pltpu.HBM),
        scratch_shapes=[pltpu.VMEM((BINS, 2, NVS, channels), F32), pltpu.SemaphoreType.DMA((BINS,))],
        compiler_params=pltpu.CompilerParams(vmem_limit_bytes=40 << 20),
        cost_estimate=pl.CostEstimate(flops=3 * 10**8, bytes_accessed=4 * 10**6, transcendentals=0),
        name="solve",
    )(*prepared, gram_a, gram_b)


CORE_PAIRS = [(0, 1), (1, 0), (2, 3), (3, 2)]
FAR_PAIRS = [(0, 2), (2, 0), (1, 3), (3, 1)]


def body(downgoing, upgoing):
    channels = downgoing.shape[1]
    sent = dft(downgoing[0], upgoing[0])
    sent = sent.reshape(NWT, ROWS // 4, 4, LANES)
    recv = lax.all_to_all(sent, "win", split_axis=0, concat_axis=0, tiled=True)
    recv = recv.reshape(NWT * ROWS, LANES)
    part = gram(recv)
    chip = part + lax.ppermute(part, "row", CORE_PAIRS)
    far = lax.ppermute(chip, "row", FAR_PAIRS)
    return solve(prep(recv, channels), chip, far, channels)


def solution(mesh):
    in_specs = (P("win", "row", None), P("win", None, None))
    out_specs = P("win", None, None, "row")
    return jax.shard_map(body, mesh=mesh, in_specs=in_specs, out_specs=out_specs, check_vma=False)
```

```python
import math

import jax
import jax.numpy as jnp
import numpy as np
from jax import lax
from jax.experimental import pallas as pl
from jax.experimental.pallas import tpu as pltpu
from jax.sharding import PartitionSpec as P

NCH = 3072
NT = 3072
NVS = 64
NWT = 64
NF = 256
DAMPING = 0.5
QUARTER = NT // 4
EIGHTH = NT // 8
LANES = 128
CH_TILE = 256
FOLD_ROWS = 16
VMEM_LIMIT = 60 << 20
BINS = 4
ROWS_D = 2 * BINS * 6
ROWS = ROWS_D + 2
HALF_VS = NVS // 2
F32 = jnp.float32
BF16 = jnp.bfloat16


def split_table(table):
    high = table.astype(BF16)
    low = (table - high.astype(np.float64)).astype(BF16)
    return np.concatenate([high, low], axis=0)


def dft_tables():
    scale = 1.0 / math.sqrt(NT)

    def trig(f, owners, samples):
        k = 4 * np.arange(NWT, dtype=np.int64)[owners] + 1 + f
        t = np.arange(samples, dtype=np.int64)
        angle = (k[:, None] * t[None, :] % NT).astype(np.float64) * (2.0 * math.pi / NT)
        return np.cos(angle) * scale, np.sin(angle) * scale

    tables = []
    for first in (0, 1):
        rows = []
        for f, sign, parity in ((0, 1.0, first), (2, -1.0, 1 - first)):
            cos, sin = trig(f, slice(parity, None, 2), EIGHTH)
            rows.append(np.concatenate([cos, -sign * sin], axis=1))
            rows.append(np.concatenate([-sin, -sign * cos], axis=1))
        tables.append(split_table(np.concatenate(rows, axis=0)))
    for f in (1, 3):
        cos, sin = trig(f, slice(None), QUARTER)
        tables.append(split_table(np.concatenate([cos, -sin], axis=0)))
    return np.concatenate(tables, axis=0)


CLASS_ROWS = [
    [(f, ri, first if f == 0 else 1 - first, 2) for f in (0, 2) for ri in range(2)] for first in (0, 1)
] + [[(f, ri, 0, 1) for ri in range(2)] for f in (1, 3)]


def split(x):
    high = x.astype(BF16)
    return high, (x - high.astype(F32)).astype(BF16)


def dot_nt(a, b):
    return lax.dot_general(a, b, (((1,), (1,)), ((), ())), preferred_element_type=F32)


def dot_nn(a, b):
    return lax.dot_general(a, b, (((1,), (0,)), ((), ())), preferred_element_type=F32)


def table_dot(table, high, low):
    half = table.shape[0] // 2
    both = dot_nt(table, high)
    return both[:half] + both[half:] + dot_nt(table[:half], low)


def core_index():
    return lax.rem(lax.axis_index("row"), 2)


def lane_quarters(parts):
    lane = lax.broadcasted_iota(jnp.int32, parts[0].shape, 1)
    halves = [jnp.where(lane % 64 < HALF_VS, parts[k], parts[k + 1]) for k in (0, 2)]
    return jnp.where(lane < 64, *halves)


def dft_kernel(x_hbm, up_hbm, table_hbm, o_ref, x_ref, table_ref, high_ref, low_ref, x_sem, up_sem, table_sem):
    channels = x_hbm.shape[0]
    tiles = channels // CH_TILE

    def x_copy(i):
        rows = pl.ds(pl.multiple_of(i * CH_TILE, CH_TILE), CH_TILE)
        return pltpu.make_async_copy(x_hbm.at[rows], x_ref.at[rows], x_sem.at[i])

    up_rows = pl.ds(pl.multiple_of(core_index() * HALF_VS, HALF_VS), HALF_VS)
    up_copy = pltpu.make_async_copy(up_hbm.at[up_rows], x_ref.at[pl.ds(channels, HALF_VS)], up_sem)
    table_copy = pltpu.make_async_copy(table_hbm, table_ref, table_sem)
    x_copy(0).start()
    table_copy.start()
    x_copy(1).start()
    up_copy.start()

    def fold(first, count):
        for r in range(0, count, FOLD_ROWS):
            x0, x1, x2, x3 = (
                x_ref[pl.ds(first + r, FOLD_ROWS), pl.ds(q * QUARTER, QUARTER)] for q in range(4)
            )
            sum0, sum1, dif0, dif1 = x0 + x2, x1 + x3, x0 - x2, x1 - x3
            near0, far0, near1, far1 = dif0[:, :EIGHTH], dif0[:, EIGHTH:], dif1[:, :EIGHTH], dif1[:, EIGHTH:]
            turn0, turn1 = (far0 - far1) * math.sqrt(0.5), (far0 + far1) * math.sqrt(0.5)
            folded = (near0 + turn0, near1 + turn1, near0 - turn0, near1 - turn1, sum0 - sum1, sum0 + sum1)
            col = 0
            for y in folded:
                cut = (pl.ds(r, FOLD_ROWS), pl.ds(col, y.shape[1]))
                high_ref[cut], low_ref[cut] = split(y)
                col += y.shape[1]

    def table(c):
        return table_ref[pl.ds(c * 2 * LANES, 2 * LANES), :]

    def owner_rows(row, owner, step):
        return pl.ds(row + owner * ROWS, NWT // step, stride=step * ROWS)

    def upgoing():
        fold(channels, HALF_VS)
        turned = []
        for c in range(len(CLASS_ROWS)):
            cut = (pl.ds(0, HALF_VS), pl.ds(c * QUARTER, QUARTER))
            both = dot_nt(jnp.concatenate([high_ref[cut], low_ref[cut]], axis=0), table(c))
            spec = both[:HALF_VS, :LANES] + both[:HALF_VS, LANES:] + both[HALF_VS:, :LANES]
            turned.append(jnp.concatenate([spec] * 4, axis=0).T)
        for owner in range(2):
            one, two = turned[owner], turned[1 - owner]
            o_ref[owner_rows(ROWS_D, owner, 2), :] = lane_quarters([one[:32], one[32:64], two[64:96], two[96:]])
        one, two = turned[2], turned[3]
        o_ref[owner_rows(ROWS_D + 1, 0, 1), :] = lane_quarters([one[:64], one[64:], two[:64], two[64:]])

    @pl.loop(0, tiles)
    def _(i):
        @pl.when(i == tiles - 1)
        def _():
            up_copy.wait()
            upgoing()

        x_copy(i).wait()

        @pl.when(i + 2 < tiles)
        def _():
            x_copy(i + 2).start()

        fold(pl.multiple_of(i * CH_TILE, CH_TILE), CH_TILE)

        @pl.when(i == 0)
        def _():
            table_copy.wait()

        for c, runs in enumerate(CLASS_ROWS):
            cut = (slice(None), pl.ds(c * QUARTER, QUARTER))
            spec = table_dot(table(c), high_ref[cut], low_ref[cut])
            start = 0
            for f, ri, owner, step in runs:
                for j in range(CH_TILE // LANES):
                    row = (f * 2 + ri) * 6 + i * (CH_TILE // LANES) + j
                    o_ref[owner_rows(row, owner, step), :] = spec[
                        start : start + NWT // step, j * LANES : (j + 1) * LANES
                    ]
                start += NWT // step


def dft(x, up):
    table = dft_tables()
    channels = x.shape[0]
    in_hbm = pl.BlockSpec(memory_space=pltpu.HBM)
    return pl.pallas_call(
        dft_kernel,
        out_shape=pltpu.VMEM((NWT * ROWS, LANES), F32),
        in_specs=[in_hbm, in_hbm, in_hbm],
        scratch_shapes=[
            pltpu.VMEM((channels + HALF_VS, NT), F32),
            pltpu.VMEM(table.shape, BF16),
            pltpu.VMEM((CH_TILE, NT), BF16),
            pltpu.VMEM((CH_TILE, NT), BF16),
            pltpu.SemaphoreType.DMA((channels // CH_TILE,)),
            pltpu.SemaphoreType.DMA,
            pltpu.SemaphoreType.DMA,
        ],
        compiler_params=pltpu.CompilerParams(vmem_limit_bytes=VMEM_LIMIT),
        cost_estimate=pl.CostEstimate(flops=3 * 10**9, bytes_accessed=15 * 10**6, transcendentals=0),
        name="dft",
    )(x, up, jnp.asarray(table))


def bin_rows(r_ref, f, ri):
    return jnp.concatenate(
        [r_ref[pl.ds((f * 2 + ri) * 6 + ct, NWT, stride=ROWS), :] for ct in range(6)], axis=1
    )


def bin_matrix(r_ref, f):
    return split(jnp.concatenate([bin_rows(r_ref, f, 0), bin_rows(r_ref, f, 1)], axis=0))


def gram_kernel(r_ref, g_ref):
    lane = lax.broadcasted_iota(jnp.int32, (NWT, LANES), 1)
    row = lax.broadcasted_iota(jnp.int32, (NWT, LANES), 0)
    upper = row <= lane % 64
    left = lane < 64
    packed = []
    for f in range(BINS):
        high, low = bin_matrix(r_ref, f)
        both = dot_nt(jnp.concatenate([high, low], axis=0), high)
        cross = both[LANES:]
        total = both[:LANES] + cross + cross.T
        below = pltpu.roll(total[64:], 64, 1)
        both = total[:64] + jnp.where(left, below, -below)
        swapped = pltpu.roll(both, 64, 1)
        packed.append(jnp.where(upper == left, both, swapped))
    for pair in range(BINS // 2):
        g_ref[pair] = jnp.where(left, packed[2 * pair], packed[2 * pair + 1])
        g_ref[BINS // 2 + pair] = r_ref[pl.ds(ROWS_D + pair, NWT, stride=ROWS), :]


def gram(recv):
    return pl.pallas_call(
        gram_kernel,
        out_shape=jax.ShapeDtypeStruct((BINS, NWT, LANES), F32),
        compiler_params=pltpu.CompilerParams(vmem_limit_bytes=40 << 20),
        cost_estimate=pl.CostEstimate(flops=3 * 10**8, bytes_accessed=2 * 10**6, transcendentals=0),
        name="gram",
    )(recv)


def prep_kernel(r_ref, own_ref, got_ref, high_ref, low_ref, start_ref):
    for f in range(BINS):
        high_ref[f], low_ref[f] = bin_matrix(r_ref, f)
    left = lax.broadcasted_iota(jnp.int32, (HALF_VS, LANES), 1) < 64
    first = core_index() == 0
    for pair in range(BINS // 2):
        own, got = own_ref[BINS // 2 + pair], got_ref[BINS // 2 + pair]
        for half, up in enumerate((jnp.where(first, own, got), jnp.where(first, got, own))):
            turned = jnp.concatenate([up, up], axis=0).T * (1.0 / math.sqrt(NCH))
            for k in range(2):
                re, im = turned[k * 64 : k * 64 + 32], turned[k * 64 + 32 : k * 64 + 64]
                start_ref[2 * k + pair, pl.ds(half * HALF_VS, HALF_VS)] = jnp.where(left, re, im)


def prep(recv, own, got, channels):
    matrices = pltpu.VMEM((BINS, 2 * NWT, channels), BF16)
    return pl.pallas_call(
        prep_kernel,
        out_shape=(matrices, matrices, pltpu.VMEM((BINS, NVS, LANES), F32)),
        compiler_params=pltpu.CompilerParams(vmem_limit_bytes=40 << 20),
        cost_estimate=pl.CostEstimate(flops=10**7, bytes_accessed=4 * 10**6, transcendentals=0),
        name="prep",
    )(recv, own, got)


def dot3(a, b_h, b_l):
    a_h, a_l = split(a)
    return dot_nn(a_h, b_h) + dot_nn(a_l, b_h) + dot_nn(a_h, b_l)


def row_dot(a, b):
    return jnp.sum(a * b, axis=1, keepdims=True)


def solve_kernel(high_ref, low_ref, start_ref, ga_ref, gb_ref, o_hbm, o_ref, o_sem):
    lane = lax.broadcasted_iota(jnp.int32, (NWT, LANES), 1)
    row = lax.broadcasted_iota(jnp.int32, (NWT, LANES), 0)
    col = lane % 64
    left = lane < 64
    grams = []
    for pair in range(BINS // 2):
        packed = ga_ref[pair] + gb_ref[pair]
        turned = jnp.concatenate([packed, packed], axis=0).T
        other = pltpu.roll(packed, 64, 1)
        for half in range(2):
            here = jnp.where(left == (half == 0), packed, other)
            there = turned[half * 64 : half * 64 + 64]
            real = jnp.where(row <= col, here, there)
            imag = jnp.where(row > col, here, jnp.where(row == col, 0.0, -there))
            top = jnp.where(left, real, imag)
            bottom = jnp.where(left, -imag, real)
            grams.append(split(jnp.concatenate([top, bottom], axis=0)))
    starts = [start_ref[f] for f in range(BINS)]

    def times_gram(ys):
        return [dot3(y, *g) for y, g in zip(ys, grams)]

    res = starts
    res_g = times_gram(res)
    res_gg = times_gram(res_g)
    copies = []
    for f in range(BINS):
        dir0, dir0_g, dir0_gg = res[f], res_g[f], res_gg[f]
        norm0 = row_dot(dir0, dir0_g)
        img = dir0_g * (1.0 / NCH) + DAMPING * dir0
        img_g = dir0_gg * (1.0 / NCH) + DAMPING * dir0_g
        step0 = norm0 / row_dot(dir0_g, img)
        res1 = dir0 - step0 * img
        res1_g = dir0_g - step0 * img_g
        norm1 = row_dot(res1, res1_g)
        ratio = norm1 / norm0
        dir1 = res1 + ratio * dir0
        dir1_g = res1_g + ratio * dir0_g
        img1 = dir1_g * (1.0 / NCH) + DAMPING * dir1
        step1 = norm1 / row_dot(dir1_g, img1)
        filt = (step0 * dir0 + step1 * dir1) * math.sqrt(NCH / NWT)
        turned = pltpu.roll(filt, 64, 1)
        lhs_h, lhs_l = split(jnp.concatenate([filt, jnp.where(left, turned, -turned)], axis=0))
        both = dot_nn(jnp.concatenate([lhs_h, lhs_l], axis=0), high_ref[f])
        out = both[:LANES] + both[LANES:] + dot_nn(lhs_h, low_ref[f])
        o_ref[f, 0] = out[:64]
        o_ref[f, 1] = out[64:]
        copies.append(pltpu.make_async_copy(o_ref.at[f], o_hbm.at[f], o_sem.at[f]))
        copies[f].start()
    for copy in copies:
        copy.wait()


def solve(prepared, gram_a, gram_b, channels):
    return pl.pallas_call(
        solve_kernel,
        out_shape=jax.ShapeDtypeStruct((BINS, 2, NVS, channels), F32),
        out_specs=pl.BlockSpec(memory_space=pltpu.HBM),
        scratch_shapes=[pltpu.VMEM((BINS, 2, NVS, channels), F32), pltpu.SemaphoreType.DMA((BINS,))],
        compiler_params=pltpu.CompilerParams(vmem_limit_bytes=40 << 20),
        cost_estimate=pl.CostEstimate(flops=3 * 10**8, bytes_accessed=4 * 10**6, transcendentals=0),
        name="solve",
    )(*prepared, gram_a, gram_b)


CORE_PAIRS = [(0, 1), (1, 0), (2, 3), (3, 2)]
FAR_PAIRS = [(0, 2), (2, 0), (1, 3), (3, 1)]


def finish(recv, part, channels):
    got = lax.ppermute(part, "row", CORE_PAIRS)
    chip = part[: BINS // 2] + got[: BINS // 2]
    far = lax.ppermute(chip, "row", FAR_PAIRS)
    return solve(prep(recv, part, got, channels), chip, far, channels)


def body(downgoing, upgoing):
    channels = downgoing.shape[1]
    sent = dft(downgoing[0], upgoing[0])
    sent = sent.reshape(NWT, ROWS // 2, 2, LANES)
    recv = lax.all_to_all(sent, "win", split_axis=0, concat_axis=0, tiled=True)
    recv = recv.reshape(NWT * ROWS, LANES)
    return finish(recv, gram(recv), channels)


def solution(mesh):
    in_specs = (P("win", "row", None), P("win", None, None))
    out_specs = P("win", None, None, "row")
    return jax.shard_map(body, mesh=mesh, in_specs=in_specs, out_specs=out_specs, check_vma=False)
```

```python
import math

import jax
import jax.numpy as jnp
import numpy as np
from jax import lax
from jax.experimental import pallas as pl
from jax.experimental.pallas import tpu as pltpu
from jax.sharding import PartitionSpec as P

NCH = 3072
NT = 3072
NVS = 64
NWT = 64
NF = 256
DAMPING = 0.5
QUARTER = NT // 4
EIGHTH = NT // 8
LANES = 128
CH_TILE = 256
FOLD_ROWS = 16
VMEM_LIMIT = 60 << 20
BINS = 4
ROWS_D = 2 * BINS * 6
ROWS = ROWS_D + 2
HALF_VS = NVS // 2
F32 = jnp.float32
BF16 = jnp.bfloat16


def split_table(table):
    high = table.astype(BF16)
    low = (table - high.astype(np.float64)).astype(BF16)
    return np.concatenate([high, low], axis=0)


def dft_tables():
    scale = 1.0 / math.sqrt(NT)

    def trig(f, owners, samples):
        k = 4 * np.arange(NWT, dtype=np.int64)[owners] + 1 + f
        t = np.arange(samples, dtype=np.int64)
        angle = (k[:, None] * t[None, :] % NT).astype(np.float64) * (2.0 * math.pi / NT)
        return np.cos(angle) * scale, np.sin(angle) * scale

    tables = []
    for first in (0, 1):
        rows = []
        for f, sign, parity in ((0, 1.0, first), (2, -1.0, 1 - first)):
            cos, sin = trig(f, slice(parity, None, 2), EIGHTH)
            rows.append(np.concatenate([cos, -sign * sin], axis=1))
            rows.append(np.concatenate([-sin, -sign * cos], axis=1))
        tables.append(split_table(np.concatenate(rows, axis=0)))
    for f in (1, 3):
        cos, sin = trig(f, slice(None), QUARTER)
        tables.append(split_table(np.concatenate([cos, -sin], axis=0)))
    return np.concatenate(tables, axis=0)


CLASS_ROWS = [
    [(f, ri, first if f == 0 else 1 - first, 2) for f in (0, 2) for ri in range(2)] for first in (0, 1)
] + [[(f, ri, 0, 1) for ri in range(2)] for f in (1, 3)]


def split(x):
    high = x.astype(BF16)
    return high, (x - high.astype(F32)).astype(BF16)


def dot_nt(a, b):
    return lax.dot_general(a, b, (((1,), (1,)), ((), ())), preferred_element_type=F32)


def dot_nn(a, b):
    return lax.dot_general(a, b, (((1,), (0,)), ((), ())), preferred_element_type=F32)


def table_dot(table, high, low):
    half = table.shape[0] // 2
    both = dot_nt(table, high)
    return both[:half] + both[half:] + dot_nt(table[:half], low)


def core_index():
    return lax.rem(lax.axis_index("row"), 2)


def lane_quarters(parts):
    lane = lax.broadcasted_iota(jnp.int32, parts[0].shape, 1)
    halves = [jnp.where(lane % 64 < HALF_VS, parts[k], parts[k + 1]) for k in (0, 2)]
    return jnp.where(lane < 64, *halves)


def dft_kernel(x_hbm, up_hbm, table_hbm, o_ref, x_ref, table_ref, high_ref, low_ref, x_sem, up_sem, table_sem):
    channels = x_hbm.shape[0]
    tiles = channels // CH_TILE

    def x_copy(i):
        rows = pl.ds(pl.multiple_of(i * CH_TILE, CH_TILE), CH_TILE)
        return pltpu.make_async_copy(x_hbm.at[rows], x_ref.at[rows], x_sem.at[i])

    up_rows = pl.ds(pl.multiple_of(core_index() * HALF_VS, HALF_VS), HALF_VS)
    up_copy = pltpu.make_async_copy(up_hbm.at[up_rows], x_ref.at[pl.ds(channels, HALF_VS)], up_sem)
    table_copy = pltpu.make_async_copy(table_hbm, table_ref, table_sem)
    up_copy.start()
    table_copy.start()
    x_copy(0).start()

    def fold(first, count):
        for r in range(0, count, FOLD_ROWS):
            x0, x1, x2, x3 = (
                x_ref[pl.ds(first + r, FOLD_ROWS), pl.ds(q * QUARTER, QUARTER)] for q in range(4)
            )
            sum0, sum1, dif0, dif1 = x0 + x2, x1 + x3, x0 - x2, x1 - x3
            near0, far0, near1, far1 = dif0[:, :EIGHTH], dif0[:, EIGHTH:], dif1[:, :EIGHTH], dif1[:, EIGHTH:]
            turn0, turn1 = (far0 - far1) * math.sqrt(0.5), (far0 + far1) * math.sqrt(0.5)
            folded = (near0 + turn0, near1 + turn1, near0 - turn0, near1 - turn1, sum0 - sum1, sum0 + sum1)
            col = 0
            for y in folded:
                cut = (pl.ds(r, FOLD_ROWS), pl.ds(col, y.shape[1]))
                high_ref[cut], low_ref[cut] = split(y)
                col += y.shape[1]

    def table(c):
        return table_ref[pl.ds(c * 2 * LANES, 2 * LANES), :]

    def owner_rows(row, owner, step):
        return pl.ds(row + owner * ROWS, NWT // step, stride=step * ROWS)

    def upgoing():
        fold(channels, HALF_VS)
        turned = []
        for c in range(len(CLASS_ROWS)):
            cut = (pl.ds(0, HALF_VS), pl.ds(c * QUARTER, QUARTER))
            both = dot_nt(jnp.concatenate([high_ref[cut], low_ref[cut]], axis=0), table(c))
            spec = both[:HALF_VS, :LANES] + both[:HALF_VS, LANES:] + both[HALF_VS:, :LANES]
            turned.append(jnp.concatenate([spec] * 4, axis=0).T)
        for owner in range(2):
            one, two = turned[owner], turned[1 - owner]
            o_ref[owner_rows(ROWS_D, owner, 2), :] = lane_quarters([one[:32], one[32:64], two[64:96], two[96:]])
        one, two = turned[2], turned[3]
        o_ref[owner_rows(ROWS_D + 1, 0, 1), :] = lane_quarters([one[:64], one[64:], two[:64], two[64:]])

    up_copy.wait()
    table_copy.wait()
    x_copy(1).start()
    upgoing()

    @pl.loop(0, tiles)
    def _(i):
        x_copy(i).wait()

        @pl.when(i + 2 < tiles)
        def _():
            x_copy(i + 2).start()

        fold(pl.multiple_of(i * CH_TILE, CH_TILE), CH_TILE)

        for c, runs in enumerate(CLASS_ROWS):
            cut = (slice(None), pl.ds(c * QUARTER, QUARTER))
            spec = table_dot(table(c), high_ref[cut], low_ref[cut])
            start = 0
            for f, ri, owner, step in runs:
                for j in range(CH_TILE // LANES):
                    row = (f * 2 + ri) * 6 + i * (CH_TILE // LANES) + j
                    o_ref[owner_rows(row, owner, step), :] = spec[
                        start : start + NWT // step, j * LANES : (j + 1) * LANES
                    ]
                start += NWT // step


def dft(x, up):
    table = dft_tables()
    channels = x.shape[0]
    in_hbm = pl.BlockSpec(memory_space=pltpu.HBM)
    return pl.pallas_call(
        dft_kernel,
        out_shape=pltpu.VMEM((NWT * ROWS, LANES), F32),
        in_specs=[in_hbm, in_hbm, in_hbm],
        scratch_shapes=[
            pltpu.VMEM((channels + HALF_VS, NT), F32),
            pltpu.VMEM(table.shape, BF16),
            pltpu.VMEM((CH_TILE, NT), BF16),
            pltpu.VMEM((CH_TILE, NT), BF16),
            pltpu.SemaphoreType.DMA((channels // CH_TILE,)),
            pltpu.SemaphoreType.DMA,
            pltpu.SemaphoreType.DMA,
        ],
        compiler_params=pltpu.CompilerParams(vmem_limit_bytes=VMEM_LIMIT),
        cost_estimate=pl.CostEstimate(flops=3 * 10**9, bytes_accessed=15 * 10**6, transcendentals=0),
        name="dft",
    )(x, up, jnp.asarray(table))


def bin_rows(r_ref, f, ri):
    return jnp.concatenate(
        [r_ref[pl.ds((f * 2 + ri) * 6 + ct, NWT, stride=ROWS), :] for ct in range(6)], axis=1
    )


def bin_matrix(r_ref, f):
    return split(jnp.concatenate([bin_rows(r_ref, f, 0), bin_rows(r_ref, f, 1)], axis=0))


def gram_kernel(r_ref, g_ref):
    lane = lax.broadcasted_iota(jnp.int32, (NWT, LANES), 1)
    row = lax.broadcasted_iota(jnp.int32, (NWT, LANES), 0)
    upper = row <= lane % 64
    left = lane < 64
    packed = []
    for f in range(BINS):
        high, low = bin_matrix(r_ref, f)
        both = dot_nt(jnp.concatenate([high, low], axis=0), high)
        cross = both[LANES:]
        total = both[:LANES] + cross + cross.T
        below = pltpu.roll(total[64:], 64, 1)
        both = total[:64] + jnp.where(left, below, -below)
        swapped = pltpu.roll(both, 64, 1)
        packed.append(jnp.where(upper == left, both, swapped))
    for pair in range(BINS // 2):
        g_ref[pair] = jnp.where(left, packed[2 * pair], packed[2 * pair + 1])
        g_ref[BINS // 2 + pair] = r_ref[pl.ds(ROWS_D + pair, NWT, stride=ROWS), :]


def gram(recv):
    return pl.pallas_call(
        gram_kernel,
        out_shape=jax.ShapeDtypeStruct((BINS, NWT, LANES), F32),
        compiler_params=pltpu.CompilerParams(vmem_limit_bytes=40 << 20),
        cost_estimate=pl.CostEstimate(flops=3 * 10**8, bytes_accessed=2 * 10**6, transcendentals=0),
        name="gram",
    )(recv)


def prep_kernel(r_ref, own_ref, got_ref, high_ref, low_ref, start_ref):
    for f in range(BINS):
        high_ref[f], low_ref[f] = bin_matrix(r_ref, f)
    left = lax.broadcasted_iota(jnp.int32, (HALF_VS, LANES), 1) < 64
    first = core_index() == 0
    for pair in range(BINS // 2):
        own, got = own_ref[BINS // 2 + pair], got_ref[BINS // 2 + pair]
        for half, up in enumerate((jnp.where(first, own, got), jnp.where(first, got, own))):
            turned = jnp.concatenate([up, up], axis=0).T * (1.0 / math.sqrt(NCH))
            for k in range(2):
                re, im = turned[k * 64 : k * 64 + 32], turned[k * 64 + 32 : k * 64 + 64]
                start_ref[2 * k + pair, pl.ds(half * HALF_VS, HALF_VS)] = jnp.where(left, re, im)


def prep(recv, own, got, channels):
    matrices = pltpu.VMEM((BINS, 2 * NWT, channels), BF16)
    return pl.pallas_call(
        prep_kernel,
        out_shape=(matrices, matrices, pltpu.VMEM((BINS, NVS, LANES), F32)),
        compiler_params=pltpu.CompilerParams(vmem_limit_bytes=40 << 20),
        cost_estimate=pl.CostEstimate(flops=10**7, bytes_accessed=4 * 10**6, transcendentals=0),
        name="prep",
    )(recv, own, got)


def dot3(a, b_h, b_l):
    a_h, a_l = split(a)
    return dot_nn(a_h, b_h) + dot_nn(a_l, b_h) + dot_nn(a_h, b_l)


def row_dot(a, b):
    return jnp.sum(a * b, axis=1, keepdims=True)


def solve_kernel(high_ref, low_ref, start_ref, ga_ref, gb_ref, o_hbm, o_ref, o_sem):
    lane = lax.broadcasted_iota(jnp.int32, (NWT, LANES), 1)
    row = lax.broadcasted_iota(jnp.int32, (NWT, LANES), 0)
    col = lane % 64
    left = lane < 64
    grams = []
    for pair in range(BINS // 2):
        packed = ga_ref[pair] + gb_ref[pair]
        turned = jnp.concatenate([packed, packed], axis=0).T
        other = pltpu.roll(packed, 64, 1)
        for half in range(2):
            here = jnp.where(left == (half == 0), packed, other)
            there = turned[half * 64 : half * 64 + 64]
            real = jnp.where(row <= col, here, there)
            imag = jnp.where(row > col, here, jnp.where(row == col, 0.0, -there))
            top = jnp.where(left, real, imag)
            bottom = jnp.where(left, -imag, real)
            grams.append(split(jnp.concatenate([top, bottom], axis=0)))
    starts = [start_ref[f] for f in range(BINS)]

    def times_gram(ys):
        return [dot3(y, *g) for y, g in zip(ys, grams)]

    res = starts
    res_g = times_gram(res)
    res_gg = times_gram(res_g)
    copies = []
    for f in range(BINS):
        dir0, dir0_g, dir0_gg = res[f], res_g[f], res_gg[f]
        norm0 = row_dot(dir0, dir0_g)
        img = dir0_g * (1.0 / NCH) + DAMPING * dir0
        img_g = dir0_gg * (1.0 / NCH) + DAMPING * dir0_g
        step0 = norm0 / row_dot(dir0_g, img)
        res1 = dir0 - step0 * img
        res1_g = dir0_g - step0 * img_g
        norm1 = row_dot(res1, res1_g)
        ratio = norm1 / norm0
        dir1 = res1 + ratio * dir0
        dir1_g = res1_g + ratio * dir0_g
        img1 = dir1_g * (1.0 / NCH) + DAMPING * dir1
        step1 = norm1 / row_dot(dir1_g, img1)
        filt = (step0 * dir0 + step1 * dir1) * math.sqrt(NCH / NWT)
        turned = pltpu.roll(filt, 64, 1)
        lhs_h, lhs_l = split(jnp.concatenate([filt, jnp.where(left, turned, -turned)], axis=0))
        both = dot_nn(jnp.concatenate([lhs_h, lhs_l], axis=0), high_ref[f])
        out = both[:LANES] + both[LANES:] + dot_nn(lhs_h, low_ref[f])
        o_ref[f, 0] = out[:64]
        o_ref[f, 1] = out[64:]
        copies.append(pltpu.make_async_copy(o_ref.at[f], o_hbm.at[f], o_sem.at[f]))
        copies[f].start()
    for copy in copies:
        copy.wait()


def solve(prepared, gram_a, gram_b, channels):
    return pl.pallas_call(
        solve_kernel,
        out_shape=jax.ShapeDtypeStruct((BINS, 2, NVS, channels), F32),
        out_specs=pl.BlockSpec(memory_space=pltpu.HBM),
        scratch_shapes=[pltpu.VMEM((BINS, 2, NVS, channels), F32), pltpu.SemaphoreType.DMA((BINS,))],
        compiler_params=pltpu.CompilerParams(vmem_limit_bytes=40 << 20),
        cost_estimate=pl.CostEstimate(flops=3 * 10**8, bytes_accessed=4 * 10**6, transcendentals=0),
        name="solve",
    )(*prepared, gram_a, gram_b)


CORE_PAIRS = [(0, 1), (1, 0), (2, 3), (3, 2)]
FAR_PAIRS = [(0, 2), (2, 0), (1, 3), (3, 1)]


def finish(recv, part, channels):
    got = lax.ppermute(part, "row", CORE_PAIRS)
    chip = part[: BINS // 2] + got[: BINS // 2]
    far = lax.ppermute(chip, "row", FAR_PAIRS)
    return solve(prep(recv, part, got, channels), chip, far, channels)


def body(downgoing, upgoing):
    channels = downgoing.shape[1]
    sent = dft(downgoing[0], upgoing[0])
    sent = sent.reshape(NWT, ROWS // 2, 2, LANES)
    recv = lax.all_to_all(sent, "win", split_axis=0, concat_axis=0, tiled=True)
    recv = recv.reshape(NWT * ROWS, LANES)
    return finish(recv, gram(recv), channels)


def solution(mesh):
    in_specs = (P("win", "row", None), P("win", None, None))
    out_specs = P("win", None, None, "row")
    return jax.shard_map(body, mesh=mesh, in_specs=in_specs, out_specs=out_specs, check_vma=False)
```

```python
import math

import jax
import jax.numpy as jnp
import numpy as np
from jax import lax
from jax.experimental import pallas as pl
from jax.experimental.pallas import tpu as pltpu
from jax.sharding import PartitionSpec as P

NCH = 3072
NT = 3072
NVS = 64
NWT = 64
NF = 256
DAMPING = 0.5
QUARTER = NT // 4
EIGHTH = NT // 8
LANES = 128
CH_TILE = 256
FOLD_ROWS = 16
VMEM_LIMIT = 60 << 20
BINS = 4
ROWS_D = 2 * BINS * 6
ROWS = ROWS_D + 2
HALF_VS = NVS // 2
F32 = jnp.float32
BF16 = jnp.bfloat16


def split_table(table):
    high = table.astype(BF16)
    low = (table - high.astype(np.float64)).astype(BF16)
    return np.concatenate([high, low], axis=0)


def dft_tables():
    scale = 1.0 / math.sqrt(NT)

    def trig(f, owners, samples):
        k = 4 * np.arange(NWT, dtype=np.int64)[owners] + 1 + f
        t = np.arange(samples, dtype=np.int64)
        angle = (k[:, None] * t[None, :] % NT).astype(np.float64) * (2.0 * math.pi / NT)
        return np.cos(angle) * scale, np.sin(angle) * scale

    tables = []
    for first in (0, 1):
        rows = []
        for f, sign, parity in ((0, 1.0, first), (2, -1.0, 1 - first)):
            cos, sin = trig(f, slice(parity, None, 2), EIGHTH)
            rows.append(np.concatenate([cos, -sign * sin], axis=1))
            rows.append(np.concatenate([-sin, -sign * cos], axis=1))
        tables.append(split_table(np.concatenate(rows, axis=0)))
    for f in (1, 3):
        cos, sin = trig(f, slice(None), QUARTER)
        tables.append(split_table(np.concatenate([cos, -sin], axis=0)))
    return np.concatenate(tables, axis=0)


CLASS_ROWS = [
    [(f, ri, first if f == 0 else 1 - first, 2) for f in (0, 2) for ri in range(2)] for first in (0, 1)
] + [[(f, ri, 0, 1) for ri in range(2)] for f in (1, 3)]


def split(x):
    high = x.astype(BF16)
    return high, (x - high.astype(F32)).astype(BF16)


def dot_nt(a, b):
    return lax.dot_general(a, b, (((1,), (1,)), ((), ())), preferred_element_type=F32)


def dot_nn(a, b):
    return lax.dot_general(a, b, (((1,), (0,)), ((), ())), preferred_element_type=F32)


def table_dot(table, high, low):
    half = table.shape[0] // 2
    both = dot_nt(table, high)
    return both[:half] + both[half:] + dot_nt(table[:half], low)


def core_index():
    return lax.rem(lax.axis_index("row"), 2)


def lane_quarters(parts):
    lane = lax.broadcasted_iota(jnp.int32, parts[0].shape, 1)
    halves = [jnp.where(lane % 64 < HALF_VS, parts[k], parts[k + 1]) for k in (0, 2)]
    return jnp.where(lane < 64, *halves)


def dft_kernel(x_hbm, up_hbm, table_hbm, o_ref, x_ref, table_ref, high_ref, low_ref, x_sem, up_sem, table_sem):
    channels = x_hbm.shape[0]
    tiles = channels // CH_TILE

    def x_copy(i):
        rows = pl.ds(pl.multiple_of(i * CH_TILE, CH_TILE), CH_TILE)
        return pltpu.make_async_copy(x_hbm.at[rows], x_ref.at[rows], x_sem.at[i])

    up_rows = pl.ds(pl.multiple_of(core_index() * HALF_VS, HALF_VS), HALF_VS)
    up_copy = pltpu.make_async_copy(up_hbm.at[up_rows], x_ref.at[pl.ds(channels, HALF_VS)], up_sem)
    table_copy = pltpu.make_async_copy(table_hbm, table_ref, table_sem)
    up_copy.start()
    table_copy.start()
    x_copy(0).start()

    def fold(first, count):
        for r in range(0, count, FOLD_ROWS):
            x0, x1, x2, x3 = (
                x_ref[pl.ds(first + r, FOLD_ROWS), pl.ds(q * QUARTER, QUARTER)] for q in range(4)
            )
            sum0, sum1, dif0, dif1 = x0 + x2, x1 + x3, x0 - x2, x1 - x3
            near0, far0, near1, far1 = dif0[:, :EIGHTH], dif0[:, EIGHTH:], dif1[:, :EIGHTH], dif1[:, EIGHTH:]
            turn0, turn1 = (far0 - far1) * math.sqrt(0.5), (far0 + far1) * math.sqrt(0.5)
            folded = (near0 + turn0, near1 + turn1, near0 - turn0, near1 - turn1, sum0 - sum1, sum0 + sum1)
            col = 0
            for y in folded:
                cut = (pl.ds(r, FOLD_ROWS), pl.ds(col, y.shape[1]))
                high_ref[cut], low_ref[cut] = split(y)
                col += y.shape[1]

    def table(c):
        return table_ref[pl.ds(c * 2 * LANES, 2 * LANES), :]

    def owner_rows(row, owner, step):
        return pl.ds(row + owner * ROWS, NWT // step, stride=step * ROWS)

    def upgoing():
        fold(channels, HALF_VS)
        turned = []
        for c in range(len(CLASS_ROWS)):
            cut = (pl.ds(0, HALF_VS), pl.ds(c * QUARTER, QUARTER))
            both = dot_nt(jnp.concatenate([high_ref[cut], low_ref[cut]], axis=0), table(c))
            spec = both[:HALF_VS, :LANES] + both[:HALF_VS, LANES:] + both[HALF_VS:, :LANES]
            turned.append(jnp.concatenate([spec] * 4, axis=0).T)
        for owner in range(2):
            one, two = turned[owner], turned[1 - owner]
            o_ref[owner_rows(ROWS_D, owner, 2), :] = lane_quarters([one[:32], one[32:64], two[64:96], two[96:]])
        one, two = turned[2], turned[3]
        o_ref[owner_rows(ROWS_D + 1, 0, 1), :] = lane_quarters([one[:64], one[64:], two[:64], two[64:]])

    up_copy.wait()
    table_copy.wait()
    x_copy(1).start()
    upgoing()

    @pl.loop(0, tiles)
    def _(i):
        x_copy(i).wait()

        @pl.when(i + 2 < tiles)
        def _():
            x_copy(i + 2).start()

        fold(pl.multiple_of(i * CH_TILE, CH_TILE), CH_TILE)

        for c, runs in enumerate(CLASS_ROWS):
            cut = (slice(None), pl.ds(c * QUARTER, QUARTER))
            spec = table_dot(table(c), high_ref[cut], low_ref[cut])
            start = 0
            for f, ri, owner, step in runs:
                for j in range(CH_TILE // LANES):
                    row = (f * 2 + ri) * 6 + i * (CH_TILE // LANES) + j
                    o_ref[owner_rows(row, owner, step), :] = spec[
                        start : start + NWT // step, j * LANES : (j + 1) * LANES
                    ]
                start += NWT // step


def dft(x, up):
    table = dft_tables()
    channels = x.shape[0]
    in_hbm = pl.BlockSpec(memory_space=pltpu.HBM)
    return pl.pallas_call(
        dft_kernel,
        out_shape=pltpu.VMEM((NWT * ROWS, LANES), F32),
        in_specs=[in_hbm, in_hbm, in_hbm],
        scratch_shapes=[
            pltpu.VMEM((channels + HALF_VS, NT), F32),
            pltpu.VMEM(table.shape, BF16),
            pltpu.VMEM((CH_TILE, NT), BF16),
            pltpu.VMEM((CH_TILE, NT), BF16),
            pltpu.SemaphoreType.DMA((channels // CH_TILE,)),
            pltpu.SemaphoreType.DMA,
            pltpu.SemaphoreType.DMA,
        ],
        compiler_params=pltpu.CompilerParams(vmem_limit_bytes=VMEM_LIMIT),
        cost_estimate=pl.CostEstimate(flops=3 * 10**9, bytes_accessed=15 * 10**6, transcendentals=0),
        name="dft",
    )(x, up, jnp.asarray(table))


def bin_rows(r_ref, f, ri):
    return jnp.concatenate(
        [r_ref[pl.ds((f * 2 + ri) * 6 + ct, NWT, stride=ROWS), :] for ct in range(6)], axis=1
    )


def bin_matrix(r_ref, f):
    return split(jnp.concatenate([bin_rows(r_ref, f, 0), bin_rows(r_ref, f, 1)], axis=0))


def gram_kernel(r_ref, g_ref):
    lane = lax.broadcasted_iota(jnp.int32, (NWT, LANES), 1)
    row = lax.broadcasted_iota(jnp.int32, (NWT, LANES), 0)
    upper = row <= lane % 64
    left = lane < 64
    packed = []
    for f in range(BINS):
        high, low = bin_matrix(r_ref, f)
        both = dot_nt(jnp.concatenate([high, low], axis=0), high)
        cross = both[LANES:]
        total = both[:LANES] + cross + cross.T
        below = pltpu.roll(total[64:], 64, 1)
        both = total[:64] + jnp.where(left, below, -below)
        swapped = pltpu.roll(both, 64, 1)
        packed.append(jnp.where(upper == left, both, swapped))
    for pair in range(BINS // 2):
        g_ref[pair] = jnp.where(left, packed[2 * pair], packed[2 * pair + 1])
        g_ref[BINS // 2 + pair] = r_ref[pl.ds(ROWS_D + pair, NWT, stride=ROWS), :]


def gram(recv):
    return pl.pallas_call(
        gram_kernel,
        out_shape=jax.ShapeDtypeStruct((BINS, NWT, LANES), F32),
        compiler_params=pltpu.CompilerParams(vmem_limit_bytes=40 << 20),
        cost_estimate=pl.CostEstimate(flops=3 * 10**8, bytes_accessed=2 * 10**6, transcendentals=0),
        name="gram",
    )(recv)


def on_channels(y, high, low):
    left = lax.broadcasted_iota(jnp.int32, y.shape, 1) < 64
    turned = pltpu.roll(y, 64, 1)
    y_high, y_low = split(jnp.concatenate([y, jnp.where(left, turned, -turned)], axis=0))
    both = dot_nn(jnp.concatenate([y_high, y_low], axis=0), high)
    return both[:LANES] + both[LANES:] + dot_nn(y_high, low)


def prep_kernel(r_ref, own_ref, got_ref, high_ref, low_ref, start_ref, rhs_ref):
    for f in range(BINS):
        high_ref[f], low_ref[f] = bin_matrix(r_ref, f)
    left = lax.broadcasted_iota(jnp.int32, (HALF_VS, LANES), 1) < 64
    first = core_index() == 0
    for pair in range(BINS // 2):
        own, got = own_ref[BINS // 2 + pair], got_ref[BINS // 2 + pair]
        for half, up in enumerate((jnp.where(first, own, got), jnp.where(first, got, own))):
            turned = jnp.concatenate([up, up], axis=0).T * (1.0 / math.sqrt(NCH))
            for k in range(2):
                re, im = turned[k * 64 : k * 64 + 32], turned[k * 64 + 32 : k * 64 + 64]
                start_ref[2 * k + pair, pl.ds(half * HALF_VS, HALF_VS)] = jnp.where(left, re, im)
    for f in range(BINS):
        rhs_ref[f] = on_channels(start_ref[f], high_ref[f], low_ref[f])


def prep(recv, own, got, channels):
    matrices = pltpu.VMEM((BINS, 2 * NWT, channels), BF16)
    return pl.pallas_call(
        prep_kernel,
        out_shape=(
            matrices,
            matrices,
            pltpu.VMEM((BINS, NVS, LANES), F32),
            pltpu.VMEM((BINS, 2 * NVS, channels), F32),
        ),
        compiler_params=pltpu.CompilerParams(vmem_limit_bytes=40 << 20),
        cost_estimate=pl.CostEstimate(flops=10**7, bytes_accessed=4 * 10**6, transcendentals=0),
        name="prep",
    )(recv, own, got)


def dot3(a, b_h, b_l):
    a_h, a_l = split(a)
    return dot_nn(a_h, b_h) + dot_nn(a_l, b_h) + dot_nn(a_h, b_l)


def row_dot(a, b):
    return jnp.sum(a * b, axis=1, keepdims=True)


def solve_kernel(high_ref, low_ref, start_ref, rhs_ref, ga_ref, gb_ref, o_hbm, o_ref, o_sem):
    lane = lax.broadcasted_iota(jnp.int32, (NWT, LANES), 1)
    row = lax.broadcasted_iota(jnp.int32, (NWT, LANES), 0)
    col = lane % 64
    left = lane < 64
    grams = []
    for pair in range(BINS // 2):
        packed = ga_ref[pair] + gb_ref[pair]
        turned = jnp.concatenate([packed, packed], axis=0).T
        other = pltpu.roll(packed, 64, 1)
        for half in range(2):
            here = jnp.where(left == (half == 0), packed, other)
            there = turned[half * 64 : half * 64 + 64]
            real = jnp.where(row <= col, here, there)
            imag = jnp.where(row > col, here, jnp.where(row == col, 0.0, -there))
            top = jnp.where(left, real, imag)
            bottom = jnp.where(left, -imag, real)
            grams.append(split(jnp.concatenate([top, bottom], axis=0)))
    starts = [start_ref[f] for f in range(BINS)]

    def times_gram(ys):
        return [dot3(y, *g) for y, g in zip(ys, grams)]

    res = starts
    res_g = times_gram(res)
    res_gg = times_gram(res_g)
    products = [on_channels(res_g[f], high_ref[f], low_ref[f]) for f in range(BINS)]
    copies = []
    for f in range(BINS):
        dir0, dir0_g, dir0_gg = res[f], res_g[f], res_gg[f]
        norm0 = row_dot(dir0, dir0_g)
        img = dir0_g * (1.0 / NCH) + DAMPING * dir0
        img_g = dir0_gg * (1.0 / NCH) + DAMPING * dir0_g
        step0 = norm0 / row_dot(dir0_g, img)
        res1 = dir0 - step0 * img
        res1_g = dir0_g - step0 * img_g
        norm1 = row_dot(res1, res1_g)
        ratio = norm1 / norm0
        dir1 = res1 + ratio * dir0
        dir1_g = res1_g + ratio * dir0_g
        img1 = dir1_g * (1.0 / NCH) + DAMPING * dir1
        step1 = norm1 / row_dot(dir1_g, img1)
        scale = math.sqrt(NCH / NWT)
        on_start = (step0 + step1 * (1.0 + ratio - DAMPING * step0)) * scale
        on_image = (step1 * step0) * (-scale / NCH)
        out = jnp.concatenate([on_start] * 2, axis=0) * rhs_ref[f] + jnp.concatenate([on_image] * 2, axis=0) * products[f]
        o_ref[f, 0] = out[:64]
        o_ref[f, 1] = out[64:]
        copies.append(pltpu.make_async_copy(o_ref.at[f], o_hbm.at[f], o_sem.at[f]))
        copies[f].start()
    for copy in copies:
        copy.wait()


def solve(prepared, gram_a, gram_b, channels):
    return pl.pallas_call(
        solve_kernel,
        out_shape=jax.ShapeDtypeStruct((BINS, 2, NVS, channels), F32),
        out_specs=pl.BlockSpec(memory_space=pltpu.HBM),
        scratch_shapes=[pltpu.VMEM((BINS, 2, NVS, channels), F32), pltpu.SemaphoreType.DMA((BINS,))],
        compiler_params=pltpu.CompilerParams(vmem_limit_bytes=40 << 20),
        cost_estimate=pl.CostEstimate(flops=3 * 10**8, bytes_accessed=4 * 10**6, transcendentals=0),
        name="solve",
    )(*prepared, gram_a, gram_b)


CORE_PAIRS = [(0, 1), (1, 0), (2, 3), (3, 2)]
FAR_PAIRS = [(0, 2), (2, 0), (1, 3), (3, 1)]


def finish(recv, part, channels):
    got = lax.ppermute(part, "row", CORE_PAIRS)
    chip = part[: BINS // 2] + got[: BINS // 2]
    far = lax.ppermute(chip, "row", FAR_PAIRS)
    return solve(prep(recv, part, got, channels), chip, far, channels)


def body(downgoing, upgoing):
    channels = downgoing.shape[1]
    sent = dft(downgoing[0], upgoing[0])
    sent = sent.reshape(NWT, ROWS // 2, 2, LANES)
    recv = lax.all_to_all(sent, "win", split_axis=0, concat_axis=0, tiled=True)
    recv = recv.reshape(NWT * ROWS, LANES)
    return finish(recv, gram(recv), channels)


def solution(mesh):
    in_specs = (P("win", "row", None), P("win", None, None))
    out_specs = P("win", None, None, "row")
    return jax.shard_map(body, mesh=mesh, in_specs=in_specs, out_specs=out_specs, check_vma=False)
```

```python
import functools
import math

import jax
import jax.numpy as jnp
import numpy as np
from jax import lax
from jax.experimental import pallas as pl
from jax.experimental.pallas import tpu as pltpu
from jax.sharding import PartitionSpec as P

NCH = 3072
NT = 3072
NVS = 64
NWT = 64
NF = 256
DAMPING = 0.5
QUARTER = NT // 4
EIGHTH = NT // 8
LANES = 128
CH_TILE = 256
FOLD_ROWS = 16
VMEM_LIMIT = 60 << 20
BINS = 4
ROWS_D = 2 * BINS * 6
ROWS = ROWS_D + 2
HALF_VS = NVS // 2
F32 = jnp.float32
BF16 = jnp.bfloat16


def split_table(table):
    high = table.astype(BF16)
    low = (table - high.astype(np.float64)).astype(BF16)
    return np.concatenate([high, low], axis=0)


def dft_tables():
    scale = 1.0 / math.sqrt(NT)

    def trig(f, owners, samples):
        k = 4 * np.arange(NWT, dtype=np.int64)[owners] + 1 + f
        t = np.arange(samples, dtype=np.int64)
        angle = (k[:, None] * t[None, :] % NT).astype(np.float64) * (2.0 * math.pi / NT)
        return np.cos(angle) * scale, np.sin(angle) * scale

    tables = []
    for first in (0, 1):
        rows = []
        for f, sign, parity in ((0, 1.0, first), (2, -1.0, 1 - first)):
            cos, sin = trig(f, slice(parity, None, 2), EIGHTH)
            rows.append(np.concatenate([cos, -sign * sin], axis=1))
            rows.append(np.concatenate([-sin, -sign * cos], axis=1))
        tables.append(split_table(np.concatenate(rows, axis=0)))
    for f in (1, 3):
        cos, sin = trig(f, slice(None), QUARTER)
        tables.append(split_table(np.concatenate([cos, -sin], axis=0)))
    return np.concatenate(tables, axis=0)


CLASS_ROWS = [
    [(f, ri, first if f == 0 else 1 - first, 2) for f in (0, 2) for ri in range(2)] for first in (0, 1)
] + [[(f, ri, 0, 1) for ri in range(2)] for f in (1, 3)]


def split(x):
    high = x.astype(BF16)
    return high, (x - high.astype(F32)).astype(BF16)


def dot_nt(a, b):
    return lax.dot_general(a, b, (((1,), (1,)), ((), ())), preferred_element_type=F32)


def dot_nn(a, b):
    return lax.dot_general(a, b, (((1,), (0,)), ((), ())), preferred_element_type=F32)


def table_dot(table, high, low):
    half = table.shape[0] // 2
    both = dot_nt(table, high)
    return both[:half] + both[half:] + dot_nt(table[:half], low)


def core_index():
    return lax.rem(lax.axis_index("row"), 2)


def lane_quarters(parts):
    lane = lax.broadcasted_iota(jnp.int32, parts[0].shape, 1)
    halves = [jnp.where(lane % 64 < HALF_VS, parts[k], parts[k + 1]) for k in (0, 2)]
    return jnp.where(lane < 64, *halves)


def dft_kernel(x_hbm, up_hbm, table_hbm, o_ref, x_ref, table_ref, high_ref, low_ref, x_sem, up_sem, table_sem):
    channels = x_hbm.shape[0]
    tiles = channels // CH_TILE

    def x_copy(i):
        rows = pl.ds(pl.multiple_of(i * CH_TILE, CH_TILE), CH_TILE)
        return pltpu.make_async_copy(x_hbm.at[rows], x_ref.at[rows], x_sem.at[i])

    up_rows = pl.ds(pl.multiple_of(core_index() * HALF_VS, HALF_VS), HALF_VS)
    up_copy = pltpu.make_async_copy(up_hbm.at[up_rows], x_ref.at[pl.ds(channels, HALF_VS)], up_sem)
    table_copy = pltpu.make_async_copy(table_hbm, table_ref, table_sem)
    up_copy.start()
    table_copy.start()
    x_copy(0).start()

    def fold(first, count):
        for r in range(0, count, FOLD_ROWS):
            x0, x1, x2, x3 = (
                x_ref[pl.ds(first + r, FOLD_ROWS), pl.ds(q * QUARTER, QUARTER)] for q in range(4)
            )
            sum0, sum1, dif0, dif1 = x0 + x2, x1 + x3, x0 - x2, x1 - x3
            near0, far0, near1, far1 = dif0[:, :EIGHTH], dif0[:, EIGHTH:], dif1[:, :EIGHTH], dif1[:, EIGHTH:]
            turn0, turn1 = (far0 - far1) * math.sqrt(0.5), (far0 + far1) * math.sqrt(0.5)
            folded = (near0 + turn0, near1 + turn1, near0 - turn0, near1 - turn1, sum0 - sum1, sum0 + sum1)
            col = 0
            for y in folded:
                cut = (pl.ds(r, FOLD_ROWS), pl.ds(col, y.shape[1]))
                high_ref[cut], low_ref[cut] = split(y)
                col += y.shape[1]

    def table(c):
        return table_ref[pl.ds(c * 2 * LANES, 2 * LANES), :]

    def owner_rows(row, owner, step):
        return pl.ds(row + owner * ROWS, NWT // step, stride=step * ROWS)

    def upgoing():
        fold(channels, HALF_VS)
        turned = []
        for c in range(len(CLASS_ROWS)):
            cut = (pl.ds(0, HALF_VS), pl.ds(c * QUARTER, QUARTER))
            both = dot_nt(jnp.concatenate([high_ref[cut], low_ref[cut]], axis=0), table(c))
            spec = both[:HALF_VS, :LANES] + both[:HALF_VS, LANES:] + both[HALF_VS:, :LANES]
            turned.append(jnp.concatenate([spec] * 4, axis=0).T)
        for owner in range(2):
            one, two = turned[owner], turned[1 - owner]
            o_ref[owner_rows(ROWS_D, owner, 2), :] = lane_quarters([one[:32], one[32:64], two[64:96], two[96:]])
        one, two = turned[2], turned[3]
        o_ref[owner_rows(ROWS_D + 1, 0, 1), :] = lane_quarters([one[:64], one[64:], two[:64], two[64:]])

    up_copy.wait()
    table_copy.wait()
    x_copy(1).start()
    upgoing()

    @pl.loop(0, tiles)
    def _(i):
        x_copy(i).wait()

        @pl.when(i + 2 < tiles)
        def _():
            x_copy(i + 2).start()

        fold(pl.multiple_of(i * CH_TILE, CH_TILE), CH_TILE)

        for c, runs in enumerate(CLASS_ROWS):
            cut = (slice(None), pl.ds(c * QUARTER, QUARTER))
            spec = table_dot(table(c), high_ref[cut], low_ref[cut])
            start = 0
            for f, ri, owner, step in runs:
                for j in range(CH_TILE // LANES):
                    row = (f * 2 + ri) * 6 + i * (CH_TILE // LANES) + j
                    o_ref[owner_rows(row, owner, step), :] = spec[
                        start : start + NWT // step, j * LANES : (j + 1) * LANES
                    ]
                start += NWT // step


def dft(x, up):
    table = dft_tables()
    channels = x.shape[0]
    in_hbm = pl.BlockSpec(memory_space=pltpu.HBM)
    return pl.pallas_call(
        dft_kernel,
        out_shape=pltpu.VMEM((NWT * ROWS, LANES), F32),
        in_specs=[in_hbm, in_hbm, in_hbm],
        scratch_shapes=[
            pltpu.VMEM((channels + HALF_VS, NT), F32),
            pltpu.VMEM(table.shape, BF16),
            pltpu.VMEM((CH_TILE, NT), BF16),
            pltpu.VMEM((CH_TILE, NT), BF16),
            pltpu.SemaphoreType.DMA((channels // CH_TILE,)),
            pltpu.SemaphoreType.DMA,
            pltpu.SemaphoreType.DMA,
        ],
        compiler_params=pltpu.CompilerParams(vmem_limit_bytes=VMEM_LIMIT),
        cost_estimate=pl.CostEstimate(flops=3 * 10**9, bytes_accessed=15 * 10**6, transcendentals=0),
        name="dft",
    )(x, up, jnp.asarray(table))


def bin_rows(r_ref, f, ri):
    return jnp.concatenate(
        [r_ref[pl.ds((f * 2 + ri) * 6 + ct, NWT, stride=ROWS), :] for ct in range(6)], axis=1
    )


def bin_matrix(r_ref, f):
    return split(jnp.concatenate([bin_rows(r_ref, f, 0), bin_rows(r_ref, f, 1)], axis=0))


def gram_kernel(pair, r_ref, g_ref):
    lane = lax.broadcasted_iota(jnp.int32, (NWT, LANES), 1)
    row = lax.broadcasted_iota(jnp.int32, (NWT, LANES), 0)
    upper = row <= lane % 64
    left = lane < 64
    packed = []
    for f in (2 * pair, 2 * pair + 1):
        high, low = bin_matrix(r_ref, f)
        both = dot_nt(jnp.concatenate([high, low], axis=0), high)
        cross = both[LANES:]
        total = both[:LANES] + cross + cross.T
        below = pltpu.roll(total[64:], 64, 1)
        both = total[:64] + jnp.where(left, below, -below)
        swapped = pltpu.roll(both, 64, 1)
        packed.append(jnp.where(upper == left, both, swapped))
    g_ref[0] = jnp.where(left, packed[0], packed[1])
    g_ref[1] = r_ref[pl.ds(ROWS_D + pair, NWT, stride=ROWS), :]


def gram(recv):
    return [gram_pair(recv, pair) for pair in range(BINS // 2)]


def gram_pair(recv, pair):
    return pl.pallas_call(
        functools.partial(gram_kernel, pair),
        out_shape=jax.ShapeDtypeStruct((2, NWT, LANES), F32),
        compiler_params=pltpu.CompilerParams(vmem_limit_bytes=40 << 20),
        cost_estimate=pl.CostEstimate(flops=3 * 10**8, bytes_accessed=2 * 10**6, transcendentals=0),
        name=f"gram{pair}",
    )(recv)


def on_channels(y, high, low):
    left = lax.broadcasted_iota(jnp.int32, y.shape, 1) < 64
    turned = pltpu.roll(y, 64, 1)
    y_high, y_low = split(jnp.concatenate([y, jnp.where(left, turned, -turned)], axis=0))
    both = dot_nn(jnp.concatenate([y_high, y_low], axis=0), high)
    return both[:LANES] + both[LANES:] + dot_nn(y_high, low)


def prep_kernel(r_ref, own0_ref, got0_ref, own1_ref, got1_ref, high_ref, low_ref, start_ref, rhs_ref):
    for f in range(BINS):
        high_ref[f], low_ref[f] = bin_matrix(r_ref, f)
    left = lax.broadcasted_iota(jnp.int32, (HALF_VS, LANES), 1) < 64
    first = core_index() == 0
    for pair, refs in enumerate(((own0_ref, got0_ref), (own1_ref, got1_ref))):
        own, got = (ref[1] for ref in refs)
        for half, up in enumerate((jnp.where(first, own, got), jnp.where(first, got, own))):
            turned = jnp.concatenate([up, up], axis=0).T * (1.0 / math.sqrt(NCH))
            for k in range(2):
                re, im = turned[k * 64 : k * 64 + 32], turned[k * 64 + 32 : k * 64 + 64]
                start_ref[2 * k + pair, pl.ds(half * HALF_VS, HALF_VS)] = jnp.where(left, re, im)
    for f in range(BINS):
        rhs_ref[f] = on_channels(start_ref[f], high_ref[f], low_ref[f])


def prep(recv, parts, gots, channels):
    matrices = pltpu.VMEM((BINS, 2 * NWT, channels), BF16)
    return pl.pallas_call(
        prep_kernel,
        out_shape=(
            matrices,
            matrices,
            pltpu.VMEM((BINS, NVS, LANES), F32),
            pltpu.VMEM((BINS, 2 * NVS, channels), F32),
        ),
        compiler_params=pltpu.CompilerParams(vmem_limit_bytes=40 << 20),
        cost_estimate=pl.CostEstimate(flops=10**7, bytes_accessed=4 * 10**6, transcendentals=0),
        name="prep",
    )(recv, parts[0], gots[0], parts[1], gots[1])


def dot3(a, b_h, b_l):
    a_h, a_l = split(a)
    return dot_nn(a_h, b_h) + dot_nn(a_l, b_h) + dot_nn(a_h, b_l)


def row_dot(a, b):
    return jnp.sum(a * b, axis=1, keepdims=True)


def solve_kernel(high_ref, low_ref, start_ref, rhs_ref, ga0_ref, ga1_ref, gb0_ref, gb1_ref, o_hbm, o_ref, o_sem):
    lane = lax.broadcasted_iota(jnp.int32, (NWT, LANES), 1)
    row = lax.broadcasted_iota(jnp.int32, (NWT, LANES), 0)
    col = lane % 64
    left = lane < 64
    grams = []
    for ga_ref, gb_ref in ((ga0_ref, gb0_ref), (ga1_ref, gb1_ref)):
        packed = ga_ref[...] + gb_ref[...]
        turned = jnp.concatenate([packed, packed], axis=0).T
        other = pltpu.roll(packed, 64, 1)
        for half in range(2):
            here = jnp.where(left == (half == 0), packed, other)
            there = turned[half * 64 : half * 64 + 64]
            real = jnp.where(row <= col, here, there)
            imag = jnp.where(row > col, here, jnp.where(row == col, 0.0, -there))
            top = jnp.where(left, real, imag)
            bottom = jnp.where(left, -imag, real)
            grams.append(split(jnp.concatenate([top, bottom], axis=0)))
    starts = [start_ref[f] for f in range(BINS)]

    def times_gram(ys):
        return [dot3(y, *g) for y, g in zip(ys, grams)]

    res = starts
    res_g = times_gram(res)
    res_gg = times_gram(res_g)
    products = [on_channels(res_g[f], high_ref[f], low_ref[f]) for f in range(BINS)]
    copies = []
    for f in range(BINS):
        dir0, dir0_g, dir0_gg = res[f], res_g[f], res_gg[f]
        norm0 = row_dot(dir0, dir0_g)
        img = dir0_g * (1.0 / NCH) + DAMPING * dir0
        img_g = dir0_gg * (1.0 / NCH) + DAMPING * dir0_g
        step0 = norm0 / row_dot(dir0_g, img)
        res1 = dir0 - step0 * img
        res1_g = dir0_g - step0 * img_g
        norm1 = row_dot(res1, res1_g)
        ratio = norm1 / norm0
        dir1 = res1 + ratio * dir0
        dir1_g = res1_g + ratio * dir0_g
        img1 = dir1_g * (1.0 / NCH) + DAMPING * dir1
        step1 = norm1 / row_dot(dir1_g, img1)
        scale = math.sqrt(NCH / NWT)
        on_start = (step0 + step1 * (1.0 + ratio - DAMPING * step0)) * scale
        on_image = (step1 * step0) * (-scale / NCH)
        out = jnp.concatenate([on_start] * 2, axis=0) * rhs_ref[f] + jnp.concatenate([on_image] * 2, axis=0) * products[f]
        o_ref[f, 0] = out[:64]
        o_ref[f, 1] = out[64:]
        copies.append(pltpu.make_async_copy(o_ref.at[f], o_hbm.at[f], o_sem.at[f]))
        copies[f].start()
    for copy in copies:
        copy.wait()


def solve(prepared, chips, fars, channels):
    return pl.pallas_call(
        solve_kernel,
        out_shape=jax.ShapeDtypeStruct((BINS, 2, NVS, channels), F32),
        out_specs=pl.BlockSpec(memory_space=pltpu.HBM),
        scratch_shapes=[pltpu.VMEM((BINS, 2, NVS, channels), F32), pltpu.SemaphoreType.DMA((BINS,))],
        compiler_params=pltpu.CompilerParams(vmem_limit_bytes=40 << 20),
        cost_estimate=pl.CostEstimate(flops=3 * 10**8, bytes_accessed=4 * 10**6, transcendentals=0),
        name="solve",
    )(*prepared, *chips, *fars)


CORE_PAIRS = [(0, 1), (1, 0), (2, 3), (3, 2)]
FAR_PAIRS = [(0, 2), (2, 0), (1, 3), (3, 1)]


def finish(recv, parts, channels):
    gots = [lax.ppermute(part, "row", CORE_PAIRS) for part in parts]
    chips = [part[0] + got[0] for part, got in zip(parts, gots)]
    fars = [lax.ppermute(chip, "row", FAR_PAIRS) for chip in chips]
    return solve(prep(recv, parts, gots, channels), chips, fars, channels)


def body(downgoing, upgoing):
    channels = downgoing.shape[1]
    sent = dft(downgoing[0], upgoing[0])
    sent = sent.reshape(NWT, ROWS // 2, 2, LANES)
    recv = lax.all_to_all(sent, "win", split_axis=0, concat_axis=0, tiled=True)
    recv = recv.reshape(NWT * ROWS, LANES)
    return finish(recv, gram(recv), channels)


def solution(mesh):
    in_specs = (P("win", "row", None), P("win", None, None))
    out_specs = P("win", None, None, "row")
    return jax.shard_map(body, mesh=mesh, in_specs=in_specs, out_specs=out_specs, check_vma=False)
```

```python
import math

import jax
import jax.numpy as jnp
import numpy as np
from jax import lax
from jax.experimental import pallas as pl
from jax.experimental.pallas import tpu as pltpu
from jax.sharding import PartitionSpec as P

NCH = 3072
NT = 3072
NVS = 64
NWT = 64
NF = 256
DAMPING = 0.5
QUARTER = NT // 4
EIGHTH = NT // 8
LANES = 128
CH_TILE = 256
FOLD_ROWS = 16
VMEM_LIMIT = 60 << 20
BINS = 4
ROWS_D = 2 * BINS * 6
ROWS = ROWS_D + 2
HALF_VS = NVS // 2
F32 = jnp.float32
BF16 = jnp.bfloat16


def split_table(table):
    high = table.astype(BF16)
    low = (table - high.astype(np.float64)).astype(BF16)
    return np.concatenate([high, low], axis=0)


def dft_tables():
    scale = 1.0 / math.sqrt(NT)

    def trig(f, owners, samples):
        k = 4 * np.arange(NWT, dtype=np.int64)[owners] + 1 + f
        t = np.arange(samples, dtype=np.int64)
        angle = (k[:, None] * t[None, :] % NT).astype(np.float64) * (2.0 * math.pi / NT)
        return np.cos(angle) * scale, np.sin(angle) * scale

    tables = []
    for first in (0, 1):
        rows = []
        for f, sign, parity in ((0, 1.0, first), (2, -1.0, 1 - first)):
            cos, sin = trig(f, slice(parity, None, 2), EIGHTH)
            rows.append(np.concatenate([cos, -sign * sin], axis=1))
            rows.append(np.concatenate([-sin, -sign * cos], axis=1))
        tables.append(split_table(np.concatenate(rows, axis=0)))
    for f in (1, 3):
        cos, sin = trig(f, slice(None), QUARTER)
        tables.append(split_table(np.concatenate([cos, -sin], axis=0)))
    return np.concatenate(tables, axis=0)


CLASS_ROWS = [
    [(f, ri, first if f == 0 else 1 - first, 2) for f in (0, 2) for ri in range(2)] for first in (0, 1)
] + [[(f, ri, 0, 1) for ri in range(2)] for f in (1, 3)]


def split(x):
    high = x.astype(BF16)
    return high, (x - high.astype(F32)).astype(BF16)


def dot_nt(a, b):
    return lax.dot_general(a, b, (((1,), (1,)), ((), ())), preferred_element_type=F32)


def dot_nn(a, b):
    return lax.dot_general(a, b, (((1,), (0,)), ((), ())), preferred_element_type=F32)


def table_dot(table, high, low):
    half = table.shape[0] // 2
    both = dot_nt(table, high)
    return both[:half] + both[half:] + dot_nt(table[:half], low)


def core_index():
    return lax.rem(lax.axis_index("row"), 2)


def lane_quarters(parts):
    lane = lax.broadcasted_iota(jnp.int32, parts[0].shape, 1)
    halves = [jnp.where(lane % 64 < HALF_VS, parts[k], parts[k + 1]) for k in (0, 2)]
    return jnp.where(lane < 64, *halves)


def dft_kernel(x_hbm, up_hbm, table_hbm, o_ref, x_ref, table_ref, high_ref, low_ref, x_sem, up_sem, table_sem):
    channels = x_hbm.shape[0]
    tiles = channels // CH_TILE

    def x_copy(i):
        rows = pl.ds(pl.multiple_of(i * CH_TILE, CH_TILE), CH_TILE)
        return pltpu.make_async_copy(x_hbm.at[rows], x_ref.at[rows], x_sem.at[i])

    up_rows = pl.ds(pl.multiple_of(core_index() * HALF_VS, HALF_VS), HALF_VS)
    up_copy = pltpu.make_async_copy(up_hbm.at[up_rows], x_ref.at[pl.ds(channels, HALF_VS)], up_sem)
    table_copy = pltpu.make_async_copy(table_hbm, table_ref, table_sem)
    up_copy.start()
    table_copy.start()
    x_copy(0).start()

    def fold(first, count):
        for r in range(0, count, FOLD_ROWS):
            x0, x1, x2, x3 = (
                x_ref[pl.ds(first + r, FOLD_ROWS), pl.ds(q * QUARTER, QUARTER)] for q in range(4)
            )
            sum0, sum1, dif0, dif1 = x0 + x2, x1 + x3, x0 - x2, x1 - x3
            near0, far0, near1, far1 = dif0[:, :EIGHTH], dif0[:, EIGHTH:], dif1[:, :EIGHTH], dif1[:, EIGHTH:]
            turn0, turn1 = (far0 - far1) * math.sqrt(0.5), (far0 + far1) * math.sqrt(0.5)
            folded = (near0 + turn0, near1 + turn1, near0 - turn0, near1 - turn1, sum0 - sum1, sum0 + sum1)
            col = 0
            for y in folded:
                cut = (pl.ds(r, FOLD_ROWS), pl.ds(col, y.shape[1]))
                high_ref[cut], low_ref[cut] = split(y)
                col += y.shape[1]

    def table(c):
        return table_ref[pl.ds(c * 2 * LANES, 2 * LANES), :]

    def owner_rows(row, owner, step):
        return pl.ds(row + owner * ROWS, NWT // step, stride=step * ROWS)

    def upgoing():
        fold(channels, HALF_VS)
        turned = []
        for c in range(len(CLASS_ROWS)):
            cut = (pl.ds(0, HALF_VS), pl.ds(c * QUARTER, QUARTER))
            both = dot_nt(jnp.concatenate([high_ref[cut], low_ref[cut]], axis=0), table(c))
            spec = both[:HALF_VS, :LANES] + both[:HALF_VS, LANES:] + both[HALF_VS:, :LANES]
            turned.append(jnp.concatenate([spec] * 4, axis=0).T)
        for owner in range(2):
            one, two = turned[owner], turned[1 - owner]
            o_ref[owner_rows(ROWS_D, owner, 2), :] = lane_quarters([one[:32], one[32:64], two[64:96], two[96:]])
        one, two = turned[2], turned[3]
        o_ref[owner_rows(ROWS_D + 1, 0, 1), :] = lane_quarters([one[:64], one[64:], two[:64], two[64:]])

    up_copy.wait()
    table_copy.wait()
    x_copy(1).start()
    upgoing()

    @pl.loop(0, tiles)
    def _(i):
        x_copy(i).wait()

        @pl.when(i + 2 < tiles)
        def _():
            x_copy(i + 2).start()

        fold(pl.multiple_of(i * CH_TILE, CH_TILE), CH_TILE)

        for c, runs in enumerate(CLASS_ROWS):
            cut = (slice(None), pl.ds(c * QUARTER, QUARTER))
            spec = table_dot(table(c), high_ref[cut], low_ref[cut])
            start = 0
            for f, ri, owner, step in runs:
                for j in range(CH_TILE // LANES):
                    row = (f * 2 + ri) * 6 + i * (CH_TILE // LANES) + j
                    o_ref[owner_rows(row, owner, step), :] = spec[
                        start : start + NWT // step, j * LANES : (j + 1) * LANES
                    ]
                start += NWT // step


def dft(x, up):
    table = dft_tables()
    channels = x.shape[0]
    in_hbm = pl.BlockSpec(memory_space=pltpu.HBM)
    return pl.pallas_call(
        dft_kernel,
        out_shape=pltpu.VMEM((NWT * ROWS, LANES), F32),
        in_specs=[in_hbm, in_hbm, in_hbm],
        scratch_shapes=[
            pltpu.VMEM((channels + HALF_VS, NT), F32),
            pltpu.VMEM(table.shape, BF16),
            pltpu.VMEM((CH_TILE, NT), BF16),
            pltpu.VMEM((CH_TILE, NT), BF16),
            pltpu.SemaphoreType.DMA((channels // CH_TILE,)),
            pltpu.SemaphoreType.DMA,
            pltpu.SemaphoreType.DMA,
        ],
        compiler_params=pltpu.CompilerParams(vmem_limit_bytes=VMEM_LIMIT),
        cost_estimate=pl.CostEstimate(flops=3 * 10**9, bytes_accessed=15 * 10**6, transcendentals=0),
        name="dft",
    )(x, up, jnp.asarray(table))


def bin_rows(r_ref, f, ri):
    return jnp.concatenate(
        [r_ref[pl.ds((f * 2 + ri) * 6 + ct, NWT, stride=ROWS), :] for ct in range(6)], axis=1
    )


def bin_matrix(r_ref, f):
    return split(jnp.concatenate([bin_rows(r_ref, f, 0), bin_rows(r_ref, f, 1)], axis=0))


def gram_kernel(r_ref, g_ref):
    lane = lax.broadcasted_iota(jnp.int32, (NWT, LANES), 1)
    row = lax.broadcasted_iota(jnp.int32, (NWT, LANES), 0)
    upper = row <= lane % 64
    left = lane < 64
    packed = []
    for f in range(BINS):
        high, low = bin_matrix(r_ref, f)
        both = dot_nt(jnp.concatenate([high, low], axis=0), high)
        cross = both[LANES:]
        total = both[:LANES] + cross + cross.T
        below = pltpu.roll(total[64:], 64, 1)
        both = total[:64] + jnp.where(left, below, -below)
        swapped = pltpu.roll(both, 64, 1)
        packed.append(jnp.where(upper == left, both, swapped))
    for pair in range(BINS // 2):
        g_ref[pair] = jnp.where(left, packed[2 * pair], packed[2 * pair + 1])
        g_ref[BINS // 2 + pair] = r_ref[pl.ds(ROWS_D + pair, NWT, stride=ROWS), :]


def gram(recv):
    return pl.pallas_call(
        gram_kernel,
        out_shape=jax.ShapeDtypeStruct((BINS, NWT, LANES), F32),
        compiler_params=pltpu.CompilerParams(vmem_limit_bytes=40 << 20),
        cost_estimate=pl.CostEstimate(flops=3 * 10**8, bytes_accessed=2 * 10**6, transcendentals=0),
        name="gram",
    )(recv)


def on_channels(y, high, low):
    left = lax.broadcasted_iota(jnp.int32, y.shape, 1) < 64
    turned = pltpu.roll(y, 64, 1)
    y_high, y_low = split(jnp.concatenate([y, jnp.where(left, turned, -turned)], axis=0))
    both = dot_nn(jnp.concatenate([y_high, y_low], axis=0), high)
    return both[:LANES] + both[LANES:] + dot_nn(y_high, low)


def prep_kernel(r_ref, own_ref, got_ref, high_ref, low_ref, start_ref, rhs_ref):
    for f in range(BINS):
        high_ref[f], low_ref[f] = bin_matrix(r_ref, f)
    left = lax.broadcasted_iota(jnp.int32, (HALF_VS, LANES), 1) < 64
    first = core_index() == 0
    for pair in range(BINS // 2):
        own, got = own_ref[BINS // 2 + pair], got_ref[BINS // 2 + pair]
        for half, up in enumerate((jnp.where(first, own, got), jnp.where(first, got, own))):
            turned = jnp.concatenate([up, up], axis=0).T * (1.0 / math.sqrt(NCH))
            for k in range(2):
                re, im = turned[k * 64 : k * 64 + 32], turned[k * 64 + 32 : k * 64 + 64]
                start_ref[2 * k + pair, pl.ds(half * HALF_VS, HALF_VS)] = jnp.where(left, re, im)
    for f in range(BINS):
        rhs_ref[f] = on_channels(start_ref[f], high_ref[f], low_ref[f])


def prep(recv, own, got, channels):
    matrices = pltpu.VMEM((BINS, 2 * NWT, channels), BF16)
    return pl.pallas_call(
        prep_kernel,
        out_shape=(
            matrices,
            matrices,
            pltpu.VMEM((BINS, NVS, LANES), F32),
            pltpu.VMEM((BINS, 2 * NVS, channels), F32),
        ),
        compiler_params=pltpu.CompilerParams(vmem_limit_bytes=40 << 20),
        cost_estimate=pl.CostEstimate(flops=10**7, bytes_accessed=4 * 10**6, transcendentals=0),
        name="prep",
    )(recv, own, got)


def dot3(a, b_h, b_l):
    a_h, a_l = split(a)
    both = dot_nn(jnp.concatenate([a_h, a_l], axis=0), b_h)
    return both[: a.shape[0]] + both[a.shape[0] :] + dot_nn(a_h, b_l)


def row_dot(a, b):
    return jnp.sum(a * b, axis=1, keepdims=True)


def solve_kernel(high_ref, low_ref, start_ref, rhs_ref, ga_ref, gb_ref, o_hbm, o_ref, o_sem):
    lane = lax.broadcasted_iota(jnp.int32, (NWT, LANES), 1)
    row = lax.broadcasted_iota(jnp.int32, (NWT, LANES), 0)
    col = lane % 64
    left = lane < 64
    grams = []
    for pair in range(BINS // 2):
        packed = ga_ref[pair] + gb_ref[pair]
        turned = jnp.concatenate([packed, packed], axis=0).T
        other = pltpu.roll(packed, 64, 1)
        for half in range(2):
            here = jnp.where(left == (half == 0), packed, other)
            there = turned[half * 64 : half * 64 + 64]
            real = jnp.where(row <= col, here, there)
            imag = jnp.where(row > col, here, jnp.where(row == col, 0.0, -there))
            top = jnp.where(left, real, imag)
            bottom = jnp.where(left, -imag, real)
            grams.append(split(jnp.concatenate([top, bottom], axis=0)))
    starts = [start_ref[f] for f in range(BINS)]

    def times_gram(ys):
        return [dot3(y, *g) for y, g in zip(ys, grams)]

    res = starts
    res_g = times_gram(res)
    res_gg = times_gram(res_g)
    products = [on_channels(res_g[f], high_ref[f], low_ref[f]) for f in range(BINS)]
    copies = []
    for f in range(BINS):
        dir0, dir0_g, dir0_gg = res[f], res_g[f], res_gg[f]
        norm0 = row_dot(dir0, dir0_g)
        img = dir0_g * (1.0 / NCH) + DAMPING * dir0
        img_g = dir0_gg * (1.0 / NCH) + DAMPING * dir0_g
        step0 = norm0 / row_dot(dir0_g, img)
        res1 = dir0 - step0 * img
        res1_g = dir0_g - step0 * img_g
        norm1 = row_dot(res1, res1_g)
        ratio = norm1 / norm0
        dir1 = res1 + ratio * dir0
        dir1_g = res1_g + ratio * dir0_g
        img1 = dir1_g * (1.0 / NCH) + DAMPING * dir1
        step1 = norm1 / row_dot(dir1_g, img1)
        scale = math.sqrt(NCH / NWT)
        on_start = (step0 + step1 * (1.0 + ratio - DAMPING * step0)) * scale
        on_image = (step1 * step0) * (-scale / NCH)
        out = jnp.concatenate([on_start] * 2, axis=0) * rhs_ref[f] + jnp.concatenate([on_image] * 2, axis=0) * products[f]
        o_ref[f, 0] = out[:64]
        o_ref[f, 1] = out[64:]
        copies.append(pltpu.make_async_copy(o_ref.at[f], o_hbm.at[f], o_sem.at[f]))
        copies[f].start()
    for copy in copies:
        copy.wait()


def solve(prepared, gram_a, gram_b, channels):
    return pl.pallas_call(
        solve_kernel,
        out_shape=jax.ShapeDtypeStruct((BINS, 2, NVS, channels), F32),
        out_specs=pl.BlockSpec(memory_space=pltpu.HBM),
        scratch_shapes=[pltpu.VMEM((BINS, 2, NVS, channels), F32), pltpu.SemaphoreType.DMA((BINS,))],
        compiler_params=pltpu.CompilerParams(vmem_limit_bytes=40 << 20),
        cost_estimate=pl.CostEstimate(flops=3 * 10**8, bytes_accessed=4 * 10**6, transcendentals=0),
        name="solve",
    )(*prepared, gram_a, gram_b)


CORE_PAIRS = [(0, 1), (1, 0), (2, 3), (3, 2)]
FAR_PAIRS = [(0, 2), (2, 0), (1, 3), (3, 1)]


def finish(recv, part, channels):
    got = lax.ppermute(part, "row", CORE_PAIRS)
    chip = part[: BINS // 2] + got[: BINS // 2]
    far = lax.ppermute(chip, "row", FAR_PAIRS)
    return solve(prep(recv, part, got, channels), chip, far, channels)


def body(downgoing, upgoing):
    channels = downgoing.shape[1]
    sent = dft(downgoing[0], upgoing[0])
    sent = sent.reshape(NWT, ROWS // 2, 2, LANES)
    recv = lax.all_to_all(sent, "win", split_axis=0, concat_axis=0, tiled=True)
    recv = recv.reshape(NWT * ROWS, LANES)
    return finish(recv, gram(recv), channels)


def solution(mesh):
    in_specs = (P("win", "row", None), P("win", None, None))
    out_specs = P("win", None, None, "row")
    return jax.shard_map(body, mesh=mesh, in_specs=in_specs, out_specs=out_specs, check_vma=False)
```
